32 devices in a mesh: rows: 8 (over y, x, core), cols: 4 (over z).
Axes of the slice: x: 2, y: 2, z: 4, core: 2. Of those that a mesh axis runs over, the one named last changes fastest.
Arguments:
- field_real: float32 [6144, 6144], P('rows', 'cols'), may hold values from -6 to 6
- field_imag: float32 [6144, 6144], P('rows', 'cols'), may hold values from -6 to 6
- kerr_map: float32 [6144, 6144], P('rows', 'cols'), may hold values from 0.1 to 1
- pinhole: int32 [6144, 6144], P(None, ('rows', 'cols')), may hold values from 0 to 1, as said below
Outputs:
- out_real: float32 [6144, 6144], P('rows', 'cols')
- out_imag: float32 [6144, 6144], P('rows', 'cols')
- b_integral: float32 [6144, 6144], P('rows', 'cols')
The draws below stay inside these ranges and needn't reach their ends.
Inputs may be any that keep to these rules, and one draw needn't show every extreme that they name: pinhole is 1 at every far-field pixel whose frequency (indices above 3072 taken as negative, so the disc wraps to the corners) lies inside a disc about zero frequency of radius R, and 0 outside it, except within about two pixels of the disc's rim, where it may take either value; R lies between 1536 and 2048 and varies from draw to draw.
All inputs are finite; a program needn't handle non-finite values.
Results may differ from the reference program's by a relative error of at most 0.00014.
Values sent between devices are 32-bit elements; how exact they have to be, the bound alone decides.
A program may use at most 192 MiB of HBM per device.

```python
import math
import jax
import jax.numpy as jnp
from jax import lax

N = 6144


def draw_pinhole(key, part):
    base = jax.random.fold_in(key, 17)
    radius_key = jax.random.fold_in(base, 1)
    flip_key = jax.random.fold_in(base, 2)
    radius = jax.random.randint(radius_key, (), N // 4, N // 3 + 1).astype(jnp.int32)
    index = jnp.arange(N, dtype=jnp.int32)
    freq = jnp.minimum(index, N - index)
    dist = freq[:, None] * freq[:, None] + freq[None, :] * freq[None, :]
    limit = radius * radius
    inside = (dist <= limit).astype(jnp.int32)
    near_rim = jnp.abs(dist - limit) <= 4 * radius
    flips = jax.random.randint(flip_key, (N, N), 0, 2).astype(jnp.int32)
    return jnp.where(near_rim, flips, inside).astype(jnp.int32)


def block_levels(own_key, dims, split, least, high):
    loudness = 1.0
    for axis_at, blocks in split:
        steps = jax.random.uniform(jax.random.fold_in(jax.random.fold_in(own_key, 6), axis_at), (blocks,), jnp.float32, least / len(split), high / len(split))
        loudness = loudness * jnp.repeat(jnp.exp(steps), dims[axis_at] // blocks).reshape((-1,) + (1,) * (len(dims) - 1 - axis_at))
    return loudness


def scatter_about(key, shape, width, bound, split=(), held_as=jnp.bfloat16):
    gain = block_levels(key, shape, split, -0.22, 0.18) if split else 1.0
    entries = jax.random.normal(key, shape, jnp.float32) * width * gain
    return jnp.minimum(jnp.maximum(entries, -bound), bound).astype(held_as)


def setup_inputs(seed: int = 0) -> dict:
    splits = jax.random.split(jax.random.key(seed), 5)
    field_real = scatter_about(splits[0], (N, N), 0.7071, 6.0, ((0, 8), (1, 4)), jnp.float32)
    field_imag = scatter_about(splits[1], (N, N), 0.7071, 6.0, ((0, 8), (1, 4)), jnp.float32)
    kerr_map = jnp.clip(jnp.exp(math.log(1.0) - 2.3025851 * jax.random.uniform(splits[2], (N, N), jnp.float32) ** block_levels(splits[2], (N, N), ((0, 8), (1, 4)), -0.2, 0.2)), 0.1, 1.0)
    pinhole = draw_pinhole(jax.random.fold_in(splits[4], 71), 0)
    return {"field_real": field_real, "field_imag": field_imag, "kerr_map": kerr_map, "pinhole": pinhole}


def kerr_phase(real_part, imag_part, kerr_map):
    power = real_part * real_part + imag_part * imag_part
    phase = kerr_map * power
    cosine = jnp.cos(phase)
    sine = jnp.sin(phase)
    return real_part * cosine - imag_part * sine, real_part * sine + imag_part * cosine, phase


def chirp_angle():
    index = jnp.arange(N, dtype=jnp.int32)
    squares = (index * index) % (2 * N)
    total = (squares[:, None] + squares[None, :]) % (2 * N)
    return -(math.pi / N) * total.astype(jnp.float32)


def propagate(real_part, imag_part, angle):
    field = lax.complex(real_part, imag_part)
    spectrum = jnp.fft.fft2(field, norm="ortho")
    spectrum = spectrum * lax.complex(jnp.cos(angle), jnp.sin(angle))
    back = jnp.fft.ifft2(spectrum, norm="ortho")
    return jnp.real(back), jnp.imag(back)


def reference(field_real, field_imag, kerr_map, pinhole):
    angle = chirp_angle()
    real_part, imag_part, phase_one = kerr_phase(field_real, field_imag, kerr_map)
    real_part, imag_part = propagate(real_part, imag_part, angle)
    real_part, imag_part, phase_two = kerr_phase(real_part, imag_part, kerr_map)
    real_part, imag_part = propagate(real_part, imag_part, angle)
    field = lax.complex(real_part, imag_part)
    spectrum = jnp.fft.fft2(field, norm="ortho") * pinhole.astype(jnp.float32)
    image = jnp.fft.ifft2(spectrum, norm="ortho")
    image = jnp.roll(jnp.flip(image, (0, 1)), 1, (0, 1))
    return jnp.real(image), jnp.imag(image), phase_one + phase_two
```

```python
import functools
import math

import jax
import jax.numpy as jnp
import numpy as np
from jax import lax
from jax.experimental import pallas as pl
from jax.experimental.pallas import tpu as pltpu
from jax.sharding import PartitionSpec as P

RADIX = 128


def phase_pair(first, second, period):
    product = first[:, None] * second[None, :] % period
    angle = 2.0 * math.pi / period * product.astype(jnp.float32)
    return (jnp.cos(angle), jnp.sin(angle))


def complex_apply(form, real_part, imag_part, cos_table, sin_table, backward, precision):
    weight = 1.0 if backward else -1.0
    real_cos = jnp.einsum(form, real_part, cos_table, precision=precision)
    real_sin = jnp.einsum(form, real_part, sin_table, precision=precision)
    imag_cos = jnp.einsum(form, imag_part, cos_table, precision=precision)
    imag_sin = jnp.einsum(form, imag_part, sin_table, precision=precision)
    return (real_cos - weight * imag_sin, imag_cos + weight * real_sin)


def twiddle(real_part, imag_part, cos_table, sin_table, backward):
    weight = 1.0 if backward else -1.0
    return (
        real_part * cos_table - weight * imag_part * sin_table,
        imag_part * cos_table + weight * real_part * sin_table,
    )


def transform_last(real_part, imag_part, backward):
    rows_here, length = real_part.shape
    blocks = length // RADIX
    outer = jnp.arange(blocks, dtype=jnp.int32)
    inner = jnp.arange(RADIX, dtype=jnp.int32)
    real_part = real_part.reshape(rows_here, blocks, RADIX)
    imag_part = imag_part.reshape(rows_here, blocks, RADIX)
    cos_outer, sin_outer = phase_pair(outer, outer, blocks)
    real_part, imag_part = complex_apply(
        "mab,ak->mkb", real_part, imag_part, cos_outer, sin_outer, backward, lax.Precision.HIGH
    )
    cos_mid, sin_mid = phase_pair(outer, inner, length)
    real_part, imag_part = twiddle(real_part, imag_part, cos_mid, sin_mid, backward)
    cos_inner, sin_inner = phase_pair(inner, inner, RADIX)
    real_part, imag_part = complex_apply(
        "mkb,bj->mkj", real_part, imag_part, cos_inner, sin_inner, backward, lax.Precision.HIGH
    )
    scale = 1.0 / math.sqrt(length)
    real_part = jnp.transpose(real_part, (0, 2, 1)).reshape(rows_here, length) * scale
    imag_part = jnp.transpose(imag_part, (0, 2, 1)).reshape(rows_here, length) * scale
    return (real_part, imag_part)


def kerr_phase(real_part, imag_part, kerr_part):
    power = real_part * real_part + imag_part * imag_part
    phase = kerr_part * power
    cosine = jnp.cos(phase)
    sine = jnp.sin(phase)
    return (real_part * cosine - imag_part * sine, real_part * sine + imag_part * cosine, phase)


def to_tall(real_part, imag_part):
    rows_here, length = real_part.shape
    device_count = lax.axis_size(("rows", "cols"))
    each = length // device_count
    real_part = real_part.reshape(rows_here, device_count, each)
    imag_part = imag_part.reshape(rows_here, device_count, each)
    real_part, imag_part = (
        lax.all_to_all(real_part, ("rows", "cols"), split_axis=1, concat_axis=0, tiled=True),
        lax.all_to_all(imag_part, ("rows", "cols"), split_axis=1, concat_axis=0, tiled=True),
    )
    real_part = jnp.transpose(real_part.reshape(device_count, rows_here, each), (2, 0, 1))
    imag_part = jnp.transpose(imag_part.reshape(device_count, rows_here, each), (2, 0, 1))
    return (real_part.reshape(each, length), imag_part.reshape(each, length))


def from_tall(real_part, imag_part):
    each, length = real_part.shape
    device_count = lax.axis_size(("rows", "cols"))
    rows_here = length // device_count
    real_part = jnp.transpose(real_part.reshape(each, device_count, rows_here), (1, 2, 0))
    imag_part = jnp.transpose(imag_part.reshape(each, device_count, rows_here), (1, 2, 0))
    real_part, imag_part = (
        lax.all_to_all(real_part, ("rows", "cols"), split_axis=0, concat_axis=2, tiled=True),
        lax.all_to_all(imag_part, ("rows", "cols"), split_axis=0, concat_axis=2, tiled=True),
    )
    return (real_part.reshape(rows_here, length), imag_part.reshape(rows_here, length))


def chirp_line(index, length):
    square = index * index % (2 * length)
    angle = -(math.pi / length) * square.astype(jnp.float32)
    return (jnp.cos(angle), jnp.sin(angle))


def multiply(real_part, imag_part, other_real, other_imag):
    return (
        real_part * other_real - imag_part * other_imag,
        real_part * other_imag + imag_part * other_real,
    )


def spectral_pair(real_part, imag_part, table_real, table_imag, backward, precision):
    rows_here, length = real_part.shape
    blocks = length // RADIX
    outer = jnp.arange(blocks, dtype=jnp.int32)
    inner = jnp.arange(RADIX, dtype=jnp.int32)
    real_part = real_part.reshape(rows_here, blocks, RADIX)
    imag_part = imag_part.reshape(rows_here, blocks, RADIX)
    cos_outer, sin_outer = phase_pair(outer, outer, blocks)
    cos_mid, sin_mid = phase_pair(outer, inner, length)
    cos_inner, sin_inner = phase_pair(inner, inner, RADIX)
    real_part, imag_part = complex_apply(
        "mab,ak->mkb", real_part, imag_part, cos_outer, sin_outer, False, precision
    )
    real_part, imag_part = twiddle(real_part, imag_part, cos_mid, sin_mid, False)
    real_part, imag_part = complex_apply(
        "mkb,bj->mkj", real_part, imag_part, cos_inner, sin_inner, False, precision
    )
    real_part, imag_part = multiply(real_part, imag_part, table_real, table_imag)
    real_part, imag_part = complex_apply(
        "mkj,jb->mkb", real_part, imag_part, cos_inner, sin_inner, backward, precision
    )
    real_part, imag_part = twiddle(real_part, imag_part, cos_mid, sin_mid, backward)
    real_part, imag_part = complex_apply(
        "mkb,ka->mab", real_part, imag_part, cos_outer, sin_outer, backward, precision
    )
    return (real_part.reshape(rows_here, length), imag_part.reshape(rows_here, length))


def tile_to_columns(part):
    wide = lax.all_to_all(part, "rows", split_axis=1, concat_axis=0, tiled=True)
    return jnp.transpose(wide)


def columns_to_rows(real_part, imag_part):
    each, length = real_part.shape
    row_count, col_count = lax.axis_size("rows"), lax.axis_size("cols")
    device_count = row_count * col_count
    rows_here = length // device_count

    def send(part):
        part = part.reshape(each, row_count, col_count, rows_here)
        part = jnp.transpose(part, (2, 1, 3, 0)).reshape(device_count, rows_here, each)
        part = lax.all_to_all(part, ("cols", "rows"), split_axis=0, concat_axis=2, tiled=True)
        return part.reshape(rows_here, length)

    return (send(real_part), send(imag_part))


def per_device(field_real, field_imag, kerr_map, pinhole):
    real_part, imag_part, phase_one = kerr_phase(field_real, field_imag, kerr_map)
    real_part, imag_part = tile_to_columns(real_part), tile_to_columns(imag_part)
    kerr_wide = lax.all_to_all(kerr_map, "cols", split_axis=0, concat_axis=1, tiled=True)
    length, each = pinhole.shape
    blocks = length // RADIX
    scale = 1.0 / length
    split_index = (
        jnp.arange(blocks, dtype=jnp.int32)[:, None]
        + blocks * jnp.arange(RADIX, dtype=jnp.int32)[None, :]
    )
    line_cos, line_sin = chirp_line(split_index, length)
    line_cos, line_sin = line_cos * scale, line_sin * scale
    own = lax.axis_index(("rows", "cols")) * each + jnp.arange(each, dtype=jnp.int32)
    own_cos, own_sin = chirp_line(own, length)
    own_cos, own_sin = own_cos[:, None, None], own_sin[:, None, None]
    aperture = jnp.transpose(pinhole.reshape(RADIX, blocks, each), (2, 1, 0)).astype(jnp.float32)
    table_real, table_imag = multiply(line_cos[None], line_sin[None], own_cos, own_sin)
    table_real, table_imag = table_real * aperture, table_imag * aperture
    real_part, imag_part = spectral_pair(real_part, imag_part, line_cos, line_sin, True, lax.Precision.HIGHEST)
    real_part, imag_part = columns_to_rows(real_part, imag_part)
    real_part, imag_part = spectral_pair(real_part, imag_part, line_cos, line_sin, True, lax.Precision.HIGHEST)
    real_part, imag_part, phase_two = kerr_phase(real_part, imag_part, kerr_wide)
    phase_back = lax.all_to_all(phase_two, "cols", split_axis=1, concat_axis=0, tiled=True)
    real_part, imag_part = transform_last(real_part, imag_part, False)
    real_part, imag_part = to_tall(real_part, imag_part)
    real_part, imag_part = spectral_pair(real_part, imag_part, table_real, table_imag, False, lax.Precision.HIGH)
    real_part, imag_part = from_tall(real_part, imag_part)
    real_part, imag_part = transform_last(real_part, imag_part, False)
    out_real, out_imag = (
        lax.all_to_all(real_part, "cols", split_axis=1, concat_axis=0, tiled=True),
        lax.all_to_all(imag_part, "cols", split_axis=1, concat_axis=0, tiled=True),
    )
    return (out_real, out_imag, phase_one + phase_back)


LANES = 128


def as_pair(values):
    high = values.astype(np.float32).astype(jnp.bfloat16)
    low = (values - high.astype(np.float64)).astype(np.float32).astype(jnp.bfloat16)
    return np.stack([high, low])


def phase_of(product, period):
    return 2.0 * np.pi * (product % period) / period


def rows_matrix(angle, scale):
    return as_pair(np.concatenate([np.cos(angle), np.sin(angle)], axis=0) * scale)


def packed(values, tail_width=64):
    half = values.shape[-1] - LANES
    pad = [(0, 0)] * (values.ndim - 1) + [(0, tail_width - half)]
    return values[..., :LANES], np.pad(values[..., LANES:], pad)


def packed_columns(real_rows, imag_rows):
    real_main, real_tail = packed(real_rows)
    imag_main, imag_tail = packed(imag_rows)
    return np.concatenate([real_main, imag_main, real_tail, imag_tail], axis=-1)


def transposed_matrix(angle, scale):
    cosine, sine = np.cos(angle) * scale, np.sin(angle) * scale
    upper = packed_columns(cosine, sine)
    lower = packed_columns(-sine, cosine)
    return as_pair(np.concatenate([upper, lower], axis=0))


def lane_square(angle_in_out, scale):
    cosine, sine = np.cos(angle_in_out) * scale, np.sin(angle_in_out) * scale
    from_real = packed_columns(cosine, -sine)
    from_imag = packed_columns(sine, cosine)
    rows = from_real.shape[0]
    pad = np.zeros((64 - (rows - LANES), from_real.shape[1]))
    return as_pair(np.concatenate(
        [from_real[:LANES], from_imag[:LANES], from_real[LANES:], pad, from_imag[LANES:], pad], axis=0
    ))


def lane_table(angle):
    cosine, sine = np.cos(angle), -np.sin(angle)
    cos_main, cos_tail = packed(cosine)
    sin_main, sin_tail = packed(sine)
    return np.stack([
        cos_main, sin_main,
        np.concatenate([cos_tail, cos_tail], axis=-1),
        np.concatenate([-sin_tail, sin_tail], axis=-1),
    ], axis=1).astype(np.float32)


def column_table(angle):
    return np.concatenate([np.cos(angle), -np.sin(angle)], axis=1).astype(np.float32)


def sign_row():
    lane = lax.broadcasted_iota(jnp.int32, (8, LANES), 1)
    return jnp.where(lane < LANES // 2, -1.0, 1.0).astype(jnp.float32)


def swap(value):
    return pltpu.roll(value, LANES // 2, 1)


class Split:
    def __init__(self, real, imag):
        self.real, self.imag = real, imag

    def __add__(self, other):
        return Split(self.real + other.real, self.imag + other.imag)

    def __sub__(self, other):
        return Split(self.real - other.real, self.imag - other.imag)

    def turn(self, cosine, sine):
        return Split(self.real * cosine - self.imag * sine, self.real * sine + self.imag * cosine)

    def quarter(self):
        return Split(self.imag, -self.real)

    def eighth(self, half):
        return Split((self.real + self.imag) * half, (self.imag - self.real) * half)


class Joint:
    def __init__(self, both, sign):
        self.both, self.sign = both, sign

    def __add__(self, other):
        return Joint(self.both + other.both, self.sign)

    def __sub__(self, other):
        return Joint(self.both - other.both, self.sign)

    def turn(self, cosine, sine):
        return Joint(self.both * cosine + swap(self.both) * (self.sign * sine), self.sign)

    def quarter(self):
        return Joint(swap(self.both) * -self.sign, self.sign)

    def eighth(self, half):
        return self.turn(half, -half)


def short_transform(items):
    count = len(items)
    if count == 1:
        return items
    if count % 4:
        return [items[0] + items[1], items[0] - items[1]]
    quarter = count // 4
    parts = [short_transform(items[index::4]) for index in range(4)]
    out = [None] * count
    for index in range(quarter):
        turned = [parts[0][index]]
        for step in range(1, 4):
            place = step * index
            item = parts[step][index]
            if place == 0:
                turned.append(item)
            elif place * 8 == count:
                turned.append(item.eighth(math.sqrt(0.5)))
            elif place * 4 == count:
                turned.append(item.quarter())
            else:
                angle = -2.0 * math.pi * place / count
                turned.append(item.turn(math.cos(angle), math.sin(angle)))
        first, second, third, fourth = turned
        even, odd = first + third, first - third
        even_two, odd_two = second + fourth, (second - fourth).quarter()
        out[index] = even + even_two
        out[index + quarter] = odd + odd_two
        out[index + 2 * quarter] = even - even_two
        out[index + 3 * quarter] = odd - odd_two
    return out


def halves(value):
    high = value.astype(jnp.bfloat16)
    return high, (value - high.astype(jnp.float32)).astype(jnp.bfloat16)


def product(left_high, left_low, right_high, right_low, dims):
    def one(left, right):
        return lax.dot_general(left, right, (dims, ((), ())), preferred_element_type=jnp.float32)

    return one(left_high, right_high) + one(left_low, right_high) + one(left_high, right_low)


NORMAL = ((1,), (0,))
FLIPPED = ((1,), (1,))


def sine_cosine(angle):
    turns = jnp.floor(angle * (2.0 / math.pi) + 0.5)
    rest = angle - turns * 1.5703125
    rest = rest - turns * 4.837512969970703125e-4
    rest = rest - turns * 7.54978995489188216e-8
    quadrant = turns.astype(jnp.int32)
    square = rest * rest
    sine = rest + rest * square * (-1.6666654611e-1 + square * (8.3321608736e-3 + square * -1.9515295891e-4))
    cosine = 1.0 + square * (-0.5 + square * (4.166664568298827e-2 + square * (-1.388731625493765e-3 + square * 2.443315711809948e-5)))
    odd = (quadrant & 1) == 1
    flip_sine = (quadrant & 2) == 2
    flip_cosine = ((quadrant + 1) & 2) == 2
    first = jnp.where(odd, cosine, sine)
    second = jnp.where(odd, sine, cosine)
    return jnp.where(flip_sine, -first, first), jnp.where(flip_cosine, -second, second)


def across(count, steps, load, store, table=None):
    def step(at, carry):
        row = pl.multiple_of(at * 8, 8)
        sign = sign_row()
        main = short_transform([Split(load(s, 0, row), load(s, 1, row)) for s in range(count)])
        for k in range(count):
            item = main[k]
            if table is not None:
                item = item.turn(*table(k, row, False))
            store(k, 0, row, item.real)
            store(k, 1, row, item.imag)
        tail = short_transform([Joint(load(s, 2, row), sign) for s in range(count)])
        for k in range(count):
            item = tail[k]
            value = item.both
            if table is not None:
                cosine, signed = table(k, row, True)
                value = value * cosine + swap(value) * signed
            store(k, 2, row, value)
        return carry

    lax.fori_loop(0, steps, step, 0)


def lane_lookup(table_ref):
    def look(k, row, tail):
        at = 2 if tail else 0
        return table_ref[k, at:at + 1, :], table_ref[k, at + 1:at + 2, :]

    return look


def column_lookup(table_ref, count):
    def look(k, row, tail):
        cosine = jnp.broadcast_to(table_ref[pl.ds(row, 8), k:k + 1], (8, LANES))
        sine = jnp.broadcast_to(table_ref[pl.ds(row, 8), count + k:count + k + 1], (8, LANES))
        return cosine, (sine * sign_row() if tail else sine)

    return look


def column_product(matrix_ref, value):
    high, low = halves(value)
    both = product(matrix_ref[0], matrix_ref[1], high, low, NORMAL)
    outs = both.shape[0] // 2
    first, second = both[:outs], both[outs:]
    sign = sign_row()[:1]
    real = first[:, :LANES] + second[:, LANES:2 * LANES]
    imag = first[:, LANES:2 * LANES] - second[:, :LANES]
    tail = first[:, 2 * LANES:] - swap(second[:, 2 * LANES:]) * sign
    return real, imag, tail


def flipped_product(matrix_ref, value):
    high, low = halves(value)
    both = product(matrix_ref[0], matrix_ref[1], high, low, FLIPPED)
    outs = both.shape[0] // 2
    width = both.shape[1] - LANES
    real, imag = both[:outs], both[outs:]
    pieces = [real[:, LANES:], imag[:, LANES:]]
    if width < LANES // 2:
        gap = jnp.zeros((outs, LANES // 2 - width), jnp.float32)
        pieces = [pieces[0], gap, pieces[1], gap]
    return real[:, :LANES], imag[:, :LANES], jnp.concatenate(pieces, axis=1)


def joined(ref, *lead):
    return jnp.concatenate([ref[lead + (plane,)] for plane in range(3)], axis=-1)


def column_turn(parts, cosine, sine):
    real, imag, tail = parts
    sign = sign_row()[:1]
    return (
        real * cosine - imag * sine,
        real * sine + imag * cosine,
        tail * cosine + swap(tail) * (sine * sign),
    )


def pick_column(table_ref, at, rows, count):
    lane = lax.broadcasted_iota(jnp.int32, (rows, 2 * count), 1)
    table = table_ref[...]
    cosine = jnp.sum(jnp.where(lane == at, table, 0.0), axis=1, keepdims=True)
    sine = jnp.sum(jnp.where(lane == at + count, table, 0.0), axis=1, keepdims=True)
    return jnp.broadcast_to(cosine, (rows, LANES)), jnp.broadcast_to(sine, (rows, LANES))


def whole(count):
    return [pl.BlockSpec(memory_space=pltpu.VMEM)] * count


def kernel_call(body, outs, inputs, scratch):
    return pl.pallas_call(
        body,
        out_shape=outs,
        in_specs=whole(len(inputs)),
        out_specs=jax.tree.map(lambda _: pl.BlockSpec(memory_space=pltpu.VMEM), outs),
        scratch_shapes=scratch,
        compiler_params=pltpu.CompilerParams(vmem_limit_bytes=62 * 1024 * 1024),
    )(*inputs)


class Plan:
    def __init__(self, length, row_count, col_count):
        self.length, self.row_count, self.col_count = length, row_count, col_count
        self.count = row_count * col_count
        self.each = length // self.count
        reach = length // 3 + 8
        near = -(-reach // self.count)
        near = (near + 3) // 4 * 4
        steps = np.arange(self.each)
        self.kept = np.concatenate([steps[:near], steps[self.each - near:]])
        self.keep = len(self.kept)
        self.near = near
        scale = 1.0 / math.sqrt(length)
        index = np.arange(self.each)
        self.full = phase_of(np.outer(index, index), self.each)
        self.cut = phase_of(np.outer(self.kept, index), self.each)
        self.scale = scale
        twist = 2.0 * np.pi * np.outer(np.arange(self.count), index) / length
        self.lane_twist = lane_table(twist)
        self.column_twist = column_table(twist.T)
        self.tall = rows_matrix(self.full, scale)
        self.tall_cut = rows_matrix(self.cut, scale)
        self.tall_back = rows_matrix(self.cut.T, scale)
        self.flip = transposed_matrix(self.full, scale)
        self.flip_cut = transposed_matrix(self.cut, scale)
        self.square = lane_square(self.cut, scale)
        far = np.arange(self.count)[:, None] + self.count * self.kept[None, :]
        self.far_chirp = lane_table(np.pi * (far * far % (2 * length)) / length)

    def slot(self, block):
        return block % self.row_count * self.col_count + block // self.row_count


def first_kernel(plan, x_ref, matrix_ref, twist_ref, out_ref, work_ref):
    count, each = plan.count, plan.each
    part = each // plan.row_count

    def step(s, carry):
        planes = [
            jnp.concatenate([x_ref[p, plane, pl.ds(s, part, stride=count), :] for p in range(plan.row_count)], axis=0)
            for plane in range(3)
        ]
        parts = column_product(matrix_ref, jnp.concatenate(planes, axis=-1))
        cosine, sine = pick_column(twist_ref, s, each, count)
        for plane, value in enumerate(column_turn(parts, cosine, sine)):
            work_ref[s, plane] = value
        return carry

    lax.fori_loop(0, count, step, 0)

    def load(s, plane, row):
        return work_ref[s, plane, pl.ds(row, 8), :]

    def store(k, plane, row, value):
        out_ref[k, plane, pl.ds(row, 8), :] = value

    across(count, each // 8, load, store)


def second_kernel(plan, x_ref, kerr_ref, theta_ref, own_ref, flip_ref, cut_ref, lane_ref, column_ref,
                  out_ref, phase_ref, work_ref, field_ref):
    count, each = plan.count, plan.each

    def load(s, plane, row):
        return x_ref[plan.slot(s), plane, pl.ds(row, 8), :]

    def store(k, plane, row, value):
        work_ref[k, plane, pl.ds(row, 8), :] = value

    across(count, each // 8, load, store, lane_lookup(lane_ref))

    def turn(k, carry):
        for plane, value in enumerate(flipped_product(flip_ref, joined(work_ref, k))):
            field_ref[plane, pl.ds(k, each, stride=count), :] = value
        return carry

    lax.fori_loop(0, count, turn, 0)
    size = 32

    def kerr(at, carry):
        rows = pl.ds(pl.multiple_of(at * size, size), size)
        sign = sign_row()[:1]
        theta = theta_ref[rows, :]
        real, imag, tail = field_ref[0, rows, :], field_ref[1, rows, :], field_ref[2, rows, :]
        phase = kerr_ref[0, rows, :] * (real * real + imag * imag)
        phase_ref[0, rows, :] = phase
        sine, cosine = sine_cosine(phase + (theta + own_ref[0:1, :]))
        field_ref[0, rows, :] = real * cosine - imag * sine
        field_ref[1, rows, :] = real * sine + imag * cosine
        square = tail * tail
        phase = kerr_ref[1, rows, :] * (square + swap(square))
        phase_ref[1, rows, :] = phase
        sine, cosine = sine_cosine(phase + (theta + own_ref[1:2, :]))
        field_ref[2, rows, :] = tail * cosine + swap(tail) * (sine * sign)
        return carry

    lax.fori_loop(0, plan.length // size, kerr, 0)

    def again(s, plane, row):
        return field_ref[plane, pl.ds(s * each + row, 8), :]

    across(count, each // 8, again, store, column_lookup(column_ref, count))

    def send(k, carry):
        for plane, value in enumerate(column_product(cut_ref, joined(work_ref, k))):
            out_ref[k, plane] = value
        return carry

    lax.fori_loop(0, count, send, 0)


def third_kernel(plan, x_ref, matrix_ref, lane_ref, out_ref, work_ref):
    def load(s, plane, row):
        return x_ref[s, plane, pl.ds(row, 8), :]

    def store(k, plane, row, value):
        work_ref[k, plane, pl.ds(row, 8), :] = value

    across(plan.count, plan.keep // 8, load, store, lane_lookup(lane_ref))

    def send(k, carry):
        for plane, value in enumerate(flipped_product(matrix_ref, joined(work_ref, k))):
            out_ref[k, plane] = value
        return carry

    lax.fori_loop(0, plan.count, send, 0)


def fourth_kernel(plan, x_ref, mask_ref, own_ref, chirp_ref, matrix_ref, lane_ref, out_ref, work_ref):
    def step(d, carry):
        sign = sign_row()[:1]
        own_cos, own_sin = own_ref[0], own_ref[1]
        main, tail_mask = mask_ref[d, 0], mask_ref[d, 1]
        far = chirp_ref[d]
        cosine = (own_cos * far[0:1] - own_sin * far[1:2]) * main
        sine = (own_cos * far[1:2] + own_sin * far[0:1]) * main
        real, imag, tail = x_ref[d, 0], x_ref[d, 1], x_ref[d, 2]
        own_tail = own_sin * sign
        tail = tail * (own_cos * tail_mask) + swap(tail) * (own_tail * tail_mask)
        tail = tail * far[2:3] + swap(tail) * far[3:4]
        value = jnp.concatenate([real * cosine - imag * sine, real * sine + imag * cosine, tail], axis=-1)
        high, low = halves(value)
        both = product(high, low, matrix_ref[0], matrix_ref[1], NORMAL)
        real, imag, tail = both[:, :LANES], both[:, LANES:2 * LANES], both[:, 2 * LANES:]
        twist = lane_ref[d]
        work_ref[d, 0] = real * twist[0:1] - imag * twist[1:2]
        work_ref[d, 1] = real * twist[1:2] + imag * twist[0:1]
        work_ref[d, 2] = tail * twist[2:3] + swap(tail) * twist[3:4]
        return carry

    lax.fori_loop(0, plan.count, step, 0)

    def load(s, plane, row):
        return work_ref[s, plane, pl.ds(row, 8), :]

    def store(k, plane, row, value):
        out_ref[plan.slot(k), plane, pl.ds(row, 8), :] = value

    across(plan.count, plan.keep // 8, load, store)


def fifth_kernel(plan, x_ref, matrix_ref, column_ref, out_ref, work_ref):
    def step(e, carry):
        parts = column_product(matrix_ref, joined(x_ref, e))
        cosine, sine = pick_column(column_ref, e, plan.each, plan.count)
        for plane, value in enumerate(column_turn(parts, cosine, sine)):
            work_ref[e, plane] = value
        return carry

    lax.fori_loop(0, plan.count, step, 0)

    def load(s, plane, row):
        return work_ref[s, plane, pl.ds(row, 8), :]

    def store(k, plane, row, value):
        out_ref[k, plane, pl.ds(row, 8), :] = value

    across(plan.count, plan.each // 8, load, store)


def f32(*shape):
    return jax.ShapeDtypeStruct(shape, jnp.float32)


def scratch(*shape):
    return pltpu.VMEM(shape, jnp.float32)


def square_angle(index, length):
    return (math.pi / length) * (index * index % (2 * length)).astype(jnp.float32)


def fast_device(plan, field_real, field_imag, kerr_map, pinhole):
    length, count, each, keep = plan.length, plan.count, plan.each, plan.keep
    rows_here, cols_here = field_real.shape
    row_at, col_at = lax.axis_index("rows"), lax.axis_index("cols")
    own = row_at * plan.col_count + col_at
    both_axes = ("rows", "cols")
    index = jnp.arange(length, dtype=jnp.int32)
    theta = square_angle(index, length)

    phase_one = kerr_map * (field_real * field_real + field_imag * field_imag)
    down = lax.dynamic_slice(theta, (row_at * rows_here,), (rows_here,))
    along = lax.dynamic_slice(theta, (col_at * cols_here,), (cols_here,))
    angle = phase_one + (down[:, None] + along[None, :])
    cosine, sine = jnp.cos(angle), jnp.sin(angle)

    def blocks(part):
        return jnp.transpose(part.reshape(rows_here, plan.row_count, each), (1, 0, 2))

    real = blocks(field_real * cosine - field_imag * sine)
    imag = blocks(field_real * sine + field_imag * cosine)
    packed_field = jnp.stack([
        real[..., :LANES], imag[..., :LANES],
        jnp.concatenate([real[..., LANES:], imag[..., LANES:]], axis=-1),
    ], axis=1)
    field = lax.all_to_all(packed_field, "rows", split_axis=0, concat_axis=0, tiled=True)
    kerr = lax.all_to_all(kerr_map.reshape(plan.col_count, each, cols_here), "cols", split_axis=0, concat_axis=0, tiled=True)
    kerr = jnp.transpose(kerr, (0, 2, 1)).reshape(length, each)
    kerr = jnp.stack([kerr[:, :LANES], jnp.concatenate([kerr[:, LANES:], kerr[:, LANES:]], axis=-1)])

    near = plan.near

    def cut(part, axis):
        size = part.shape[axis]
        return jnp.concatenate([
            lax.slice_in_dim(part, 0, near, axis=axis), lax.slice_in_dim(part, size - near, size, axis=axis)
        ], axis=axis)

    mask = jnp.transpose(cut(pinhole.reshape(each, count, each), 0), (1, 0, 2)).astype(jnp.float32)
    mask = lax.all_to_all(mask, both_axes, split_axis=0, concat_axis=0, tiled=True)
    mask = jnp.transpose(mask, (1, 0, 2)).reshape(keep, each, count)
    mask = jnp.transpose(cut(mask, 1), (2, 0, 1))
    tail = jnp.pad(mask[..., LANES:], ((0, 0), (0, 0), (0, LANES // 2 - (keep - LANES))))
    mask = jnp.stack([mask[..., :LANES], jnp.concatenate([tail, tail], axis=-1)], axis=1)

    theta_wide = jnp.broadcast_to(theta[:, None] - math.pi / 2, (length, LANES))
    lines = lax.dynamic_slice(theta, (own * each,), (each,))
    own_theta = jnp.stack([lines[:LANES], jnp.concatenate([lines[LANES:], lines[LANES:]])])
    far = own + count * jnp.asarray(plan.kept, jnp.int32)
    far_angle = square_angle(far, length)
    own_chirp = jnp.broadcast_to(jnp.stack([jnp.cos(far_angle), -jnp.sin(far_angle)])[:, :, None], (2, keep, LANES))

    def exchange(part):
        return lax.all_to_all(part, both_axes, split_axis=0, concat_axis=0, tiled=True)

    field = kernel_call(
        functools.partial(first_kernel, plan), f32(count, 3, each, LANES),
        (field, plan.tall, plan.column_twist), [scratch(count, 3, each, LANES)],
    )
    field = exchange(field)
    field, phase_two = kernel_call(
        functools.partial(second_kernel, plan),
        (f32(count, 3, keep, LANES), f32(2, length, LANES)),
        (field, kerr, theta_wide, own_theta, plan.flip, plan.tall_cut, plan.lane_twist, plan.column_twist),
        [scratch(count, 3, each, LANES), scratch(3, length, LANES)],
    )
    field = exchange(field)
    field = kernel_call(
        functools.partial(third_kernel, plan), f32(count, 3, keep, LANES),
        (field, plan.flip_cut, plan.lane_twist), [scratch(count, 3, keep, LANES)],
    )
    field = exchange(field)
    field = kernel_call(
        functools.partial(fourth_kernel, plan), f32(count, 3, keep, LANES),
        (field, mask, own_chirp, plan.far_chirp, plan.square, plan.lane_twist), [scratch(count, 3, keep, LANES)],
    )
    field = exchange(field)
    field = kernel_call(
        functools.partial(fifth_kernel, plan), f32(count, 3, each, LANES),
        (field, plan.tall_back, plan.column_twist), [scratch(count, 3, each, LANES)],
    )
    field = field.reshape(plan.row_count, plan.col_count, 3, each, LANES)
    field = lax.all_to_all(field, "rows", split_axis=0, concat_axis=0, tiled=True)
    real = jnp.concatenate([field[:, :, 0], field[:, :, 2, :, :LANES // 2]], axis=-1)
    imag = jnp.concatenate([field[:, :, 1], field[:, :, 2, :, LANES // 2:]], axis=-1)
    out_real = jnp.transpose(real, (1, 2, 0, 3)).reshape(rows_here, cols_here)
    out_imag = jnp.transpose(imag, (1, 2, 0, 3)).reshape(rows_here, cols_here)
    phase = jnp.concatenate([phase_two[0], phase_two[1][:, :LANES // 2]], axis=-1)
    phase = jnp.transpose(phase.reshape(plan.col_count, cols_here, each), (0, 2, 1))
    phase = lax.all_to_all(phase, "cols", split_axis=0, concat_axis=0, tiled=True)
    return (out_real, out_imag, phase_one + phase.reshape(rows_here, cols_here))


def suits(length, count):
    each = length // count
    return count == 32 and each - LANES == LANES // 2


def solution(mesh):
    placed = (P("rows", "cols"), P("rows", "cols"), P("rows", "cols"), P(None, ("rows", "cols")))

    def device(field_real, field_imag, kerr_map, pinhole):
        row_count, col_count = mesh.shape["rows"], mesh.shape["cols"]
        length = pinhole.shape[0]
        if suits(length, row_count * col_count):
            plan = Plan(length, row_count, col_count)
            return fast_device(plan, field_real, field_imag, kerr_map, pinhole)
        return per_device(field_real, field_imag, kerr_map, pinhole)

    return jax.shard_map(
        device,
        mesh=mesh,
        in_specs=placed,
        out_specs=(P("rows", "cols"), P("rows", "cols"), P("rows", "cols")),
        check_vma=False,
    )
```

```python
import functools
import math

import jax
import jax.numpy as jnp
import numpy as np
from jax import lax
from jax.experimental import pallas as pl
from jax.experimental.pallas import tpu as pltpu
from jax.sharding import PartitionSpec as P

RADIX = 128


def phase_pair(first, second, period):
    product = first[:, None] * second[None, :] % period
    angle = 2.0 * math.pi / period * product.astype(jnp.float32)
    return (jnp.cos(angle), jnp.sin(angle))


def complex_apply(form, real_part, imag_part, cos_table, sin_table, backward, precision):
    weight = 1.0 if backward else -1.0
    real_cos = jnp.einsum(form, real_part, cos_table, precision=precision)
    real_sin = jnp.einsum(form, real_part, sin_table, precision=precision)
    imag_cos = jnp.einsum(form, imag_part, cos_table, precision=precision)
    imag_sin = jnp.einsum(form, imag_part, sin_table, precision=precision)
    return (real_cos - weight * imag_sin, imag_cos + weight * real_sin)


def twiddle(real_part, imag_part, cos_table, sin_table, backward):
    weight = 1.0 if backward else -1.0
    return (
        real_part * cos_table - weight * imag_part * sin_table,
        imag_part * cos_table + weight * real_part * sin_table,
    )


def transform_last(real_part, imag_part, backward):
    rows_here, length = real_part.shape
    blocks = length // RADIX
    outer = jnp.arange(blocks, dtype=jnp.int32)
    inner = jnp.arange(RADIX, dtype=jnp.int32)
    real_part = real_part.reshape(rows_here, blocks, RADIX)
    imag_part = imag_part.reshape(rows_here, blocks, RADIX)
    cos_outer, sin_outer = phase_pair(outer, outer, blocks)
    real_part, imag_part = complex_apply(
        "mab,ak->mkb", real_part, imag_part, cos_outer, sin_outer, backward, lax.Precision.HIGH
    )
    cos_mid, sin_mid = phase_pair(outer, inner, length)
    real_part, imag_part = twiddle(real_part, imag_part, cos_mid, sin_mid, backward)
    cos_inner, sin_inner = phase_pair(inner, inner, RADIX)
    real_part, imag_part = complex_apply(
        "mkb,bj->mkj", real_part, imag_part, cos_inner, sin_inner, backward, lax.Precision.HIGH
    )
    scale = 1.0 / math.sqrt(length)
    real_part = jnp.transpose(real_part, (0, 2, 1)).reshape(rows_here, length) * scale
    imag_part = jnp.transpose(imag_part, (0, 2, 1)).reshape(rows_here, length) * scale
    return (real_part, imag_part)


def kerr_phase(real_part, imag_part, kerr_part):
    power = real_part * real_part + imag_part * imag_part
    phase = kerr_part * power
    cosine = jnp.cos(phase)
    sine = jnp.sin(phase)
    return (real_part * cosine - imag_part * sine, real_part * sine + imag_part * cosine, phase)


def to_tall(real_part, imag_part):
    rows_here, length = real_part.shape
    device_count = lax.axis_size(("rows", "cols"))
    each = length // device_count
    real_part = real_part.reshape(rows_here, device_count, each)
    imag_part = imag_part.reshape(rows_here, device_count, each)
    real_part, imag_part = (
        lax.all_to_all(real_part, ("rows", "cols"), split_axis=1, concat_axis=0, tiled=True),
        lax.all_to_all(imag_part, ("rows", "cols"), split_axis=1, concat_axis=0, tiled=True),
    )
    real_part = jnp.transpose(real_part.reshape(device_count, rows_here, each), (2, 0, 1))
    imag_part = jnp.transpose(imag_part.reshape(device_count, rows_here, each), (2, 0, 1))
    return (real_part.reshape(each, length), imag_part.reshape(each, length))


def from_tall(real_part, imag_part):
    each, length = real_part.shape
    device_count = lax.axis_size(("rows", "cols"))
    rows_here = length // device_count
    real_part = jnp.transpose(real_part.reshape(each, device_count, rows_here), (1, 2, 0))
    imag_part = jnp.transpose(imag_part.reshape(each, device_count, rows_here), (1, 2, 0))
    real_part, imag_part = (
        lax.all_to_all(real_part, ("rows", "cols"), split_axis=0, concat_axis=2, tiled=True),
        lax.all_to_all(imag_part, ("rows", "cols"), split_axis=0, concat_axis=2, tiled=True),
    )
    return (real_part.reshape(rows_here, length), imag_part.reshape(rows_here, length))


def chirp_line(index, length):
    square = index * index % (2 * length)
    angle = -(math.pi / length) * square.astype(jnp.float32)
    return (jnp.cos(angle), jnp.sin(angle))


def multiply(real_part, imag_part, other_real, other_imag):
    return (
        real_part * other_real - imag_part * other_imag,
        real_part * other_imag + imag_part * other_real,
    )


def spectral_pair(real_part, imag_part, table_real, table_imag, backward, precision):
    rows_here, length = real_part.shape
    blocks = length // RADIX
    outer = jnp.arange(blocks, dtype=jnp.int32)
    inner = jnp.arange(RADIX, dtype=jnp.int32)
    real_part = real_part.reshape(rows_here, blocks, RADIX)
    imag_part = imag_part.reshape(rows_here, blocks, RADIX)
    cos_outer, sin_outer = phase_pair(outer, outer, blocks)
    cos_mid, sin_mid = phase_pair(outer, inner, length)
    cos_inner, sin_inner = phase_pair(inner, inner, RADIX)
    real_part, imag_part = complex_apply(
        "mab,ak->mkb", real_part, imag_part, cos_outer, sin_outer, False, precision
    )
    real_part, imag_part = twiddle(real_part, imag_part, cos_mid, sin_mid, False)
    real_part, imag_part = complex_apply(
        "mkb,bj->mkj", real_part, imag_part, cos_inner, sin_inner, False, precision
    )
    real_part, imag_part = multiply(real_part, imag_part, table_real, table_imag)
    real_part, imag_part = complex_apply(
        "mkj,jb->mkb", real_part, imag_part, cos_inner, sin_inner, backward, precision
    )
    real_part, imag_part = twiddle(real_part, imag_part, cos_mid, sin_mid, backward)
    real_part, imag_part = complex_apply(
        "mkb,ka->mab", real_part, imag_part, cos_outer, sin_outer, backward, precision
    )
    return (real_part.reshape(rows_here, length), imag_part.reshape(rows_here, length))


def tile_to_columns(part):
    wide = lax.all_to_all(part, "rows", split_axis=1, concat_axis=0, tiled=True)
    return jnp.transpose(wide)


def columns_to_rows(real_part, imag_part):
    each, length = real_part.shape
    row_count, col_count = lax.axis_size("rows"), lax.axis_size("cols")
    device_count = row_count * col_count
    rows_here = length // device_count

    def send(part):
        part = part.reshape(each, row_count, col_count, rows_here)
        part = jnp.transpose(part, (2, 1, 3, 0)).reshape(device_count, rows_here, each)
        part = lax.all_to_all(part, ("cols", "rows"), split_axis=0, concat_axis=2, tiled=True)
        return part.reshape(rows_here, length)

    return (send(real_part), send(imag_part))


def per_device(field_real, field_imag, kerr_map, pinhole):
    real_part, imag_part, phase_one = kerr_phase(field_real, field_imag, kerr_map)
    real_part, imag_part = tile_to_columns(real_part), tile_to_columns(imag_part)
    kerr_wide = lax.all_to_all(kerr_map, "cols", split_axis=0, concat_axis=1, tiled=True)
    length, each = pinhole.shape
    blocks = length // RADIX
    scale = 1.0 / length
    split_index = (
        jnp.arange(blocks, dtype=jnp.int32)[:, None]
        + blocks * jnp.arange(RADIX, dtype=jnp.int32)[None, :]
    )
    line_cos, line_sin = chirp_line(split_index, length)
    line_cos, line_sin = line_cos * scale, line_sin * scale
    own = lax.axis_index(("rows", "cols")) * each + jnp.arange(each, dtype=jnp.int32)
    own_cos, own_sin = chirp_line(own, length)
    own_cos, own_sin = own_cos[:, None, None], own_sin[:, None, None]
    aperture = jnp.transpose(pinhole.reshape(RADIX, blocks, each), (2, 1, 0)).astype(jnp.float32)
    table_real, table_imag = multiply(line_cos[None], line_sin[None], own_cos, own_sin)
    table_real, table_imag = table_real * aperture, table_imag * aperture
    real_part, imag_part = spectral_pair(real_part, imag_part, line_cos, line_sin, True, lax.Precision.HIGHEST)
    real_part, imag_part = columns_to_rows(real_part, imag_part)
    real_part, imag_part = spectral_pair(real_part, imag_part, line_cos, line_sin, True, lax.Precision.HIGHEST)
    real_part, imag_part, phase_two = kerr_phase(real_part, imag_part, kerr_wide)
    phase_back = lax.all_to_all(phase_two, "cols", split_axis=1, concat_axis=0, tiled=True)
    real_part, imag_part = transform_last(real_part, imag_part, False)
    real_part, imag_part = to_tall(real_part, imag_part)
    real_part, imag_part = spectral_pair(real_part, imag_part, table_real, table_imag, False, lax.Precision.HIGH)
    real_part, imag_part = from_tall(real_part, imag_part)
    real_part, imag_part = transform_last(real_part, imag_part, False)
    out_real, out_imag = (
        lax.all_to_all(real_part, "cols", split_axis=1, concat_axis=0, tiled=True),
        lax.all_to_all(imag_part, "cols", split_axis=1, concat_axis=0, tiled=True),
    )
    return (out_real, out_imag, phase_one + phase_back)


LANES = 128


def as_pair(values):
    high = values.astype(np.float32).astype(jnp.bfloat16)
    low = (values - high.astype(np.float64)).astype(np.float32).astype(jnp.bfloat16)
    return np.stack([high, low])


def phase_of(product, period):
    return 2.0 * np.pi * (product % period) / period


def rows_matrix(angle, scale):
    return as_pair(np.concatenate([np.cos(angle), np.sin(angle)], axis=0) * scale)


def packed(values, tail_width=64):
    half = values.shape[-1] - LANES
    pad = [(0, 0)] * (values.ndim - 1) + [(0, tail_width - half)]
    return values[..., :LANES], np.pad(values[..., LANES:], pad)


def packed_columns(real_rows, imag_rows):
    real_main, real_tail = packed(real_rows)
    imag_main, imag_tail = packed(imag_rows)
    return np.concatenate([real_main, imag_main, real_tail, imag_tail], axis=-1)


def transposed_matrix(angle, scale):
    cosine, sine = np.cos(angle) * scale, np.sin(angle) * scale
    upper = packed_columns(cosine, sine)
    lower = packed_columns(-sine, cosine)
    return as_pair(np.concatenate([upper, lower], axis=0))


def lane_square(angle_in_out, scale):
    cosine, sine = np.cos(angle_in_out) * scale, np.sin(angle_in_out) * scale
    from_real = packed_columns(cosine, -sine)
    from_imag = packed_columns(sine, cosine)
    rows = from_real.shape[0]
    pad = np.zeros((64 - (rows - LANES), from_real.shape[1]))
    return as_pair(np.concatenate(
        [from_real[:LANES], from_imag[:LANES], from_real[LANES:], pad, from_imag[LANES:], pad], axis=0
    ))


def lane_table(angle):
    cosine, sine = np.cos(angle), -np.sin(angle)
    cos_main, cos_tail = packed(cosine)
    sin_main, sin_tail = packed(sine)
    return np.stack([
        cos_main, sin_main,
        np.concatenate([cos_tail, cos_tail], axis=-1),
        np.concatenate([-sin_tail, sin_tail], axis=-1),
    ], axis=1).astype(np.float32)


def column_table(angle):
    return np.concatenate([np.cos(angle), -np.sin(angle)], axis=1).astype(np.float32)


def sign_row():
    lane = lax.broadcasted_iota(jnp.int32, (8, LANES), 1)
    return jnp.where(lane < LANES // 2, -1.0, 1.0).astype(jnp.float32)


def swap(value):
    return pltpu.roll(value, LANES // 2, 1)


class Split:
    def __init__(self, real, imag):
        self.real, self.imag = real, imag

    def __add__(self, other):
        return Split(self.real + other.real, self.imag + other.imag)

    def __sub__(self, other):
        return Split(self.real - other.real, self.imag - other.imag)

    def turn(self, cosine, sine):
        return Split(self.real * cosine - self.imag * sine, self.real * sine + self.imag * cosine)

    def quarter(self):
        return Split(self.imag, -self.real)

    def eighth(self, half):
        return Split((self.real + self.imag) * half, (self.imag - self.real) * half)


class Joint:
    def __init__(self, both, sign):
        self.both, self.sign = both, sign

    def __add__(self, other):
        return Joint(self.both + other.both, self.sign)

    def __sub__(self, other):
        return Joint(self.both - other.both, self.sign)

    def turn(self, cosine, sine):
        return Joint(self.both * cosine + swap(self.both) * (self.sign * sine), self.sign)

    def quarter(self):
        return Joint(swap(self.both) * -self.sign, self.sign)

    def eighth(self, half):
        return self.turn(half, -half)


def short_transform(items):
    count = len(items)
    if count == 1:
        return items
    if count % 4:
        return [items[0] + items[1], items[0] - items[1]]
    quarter = count // 4
    parts = [short_transform(items[index::4]) for index in range(4)]
    out = [None] * count
    for index in range(quarter):
        turned = [parts[0][index]]
        for step in range(1, 4):
            place = step * index
            item = parts[step][index]
            if place == 0:
                turned.append(item)
            elif place * 8 == count:
                turned.append(item.eighth(math.sqrt(0.5)))
            elif place * 4 == count:
                turned.append(item.quarter())
            else:
                angle = -2.0 * math.pi * place / count
                turned.append(item.turn(math.cos(angle), math.sin(angle)))
        first, second, third, fourth = turned
        even, odd = first + third, first - third
        even_two, odd_two = second + fourth, (second - fourth).quarter()
        out[index] = even + even_two
        out[index + quarter] = odd + odd_two
        out[index + 2 * quarter] = even - even_two
        out[index + 3 * quarter] = odd - odd_two
    return out


def halves(value):
    high = value.astype(jnp.bfloat16)
    return high, (value - high.astype(jnp.float32)).astype(jnp.bfloat16)


def product(left_high, left_low, right_high, right_low, dims):
    def one(left, right):
        return lax.dot_general(left, right, (dims, ((), ())), preferred_element_type=jnp.float32)

    return one(left_high, right_high) + one(left_low, right_high) + one(left_high, right_low)


NORMAL = ((1,), (0,))
FLIPPED = ((1,), (1,))


def sine_cosine(angle):
    turns = jnp.floor(angle * (2.0 / math.pi) + 0.5)
    rest = angle - turns * 1.5703125
    rest = rest - turns * 4.837512969970703125e-4
    rest = rest - turns * 7.54978995489188216e-8
    quadrant = turns.astype(jnp.int32)
    square = rest * rest
    sine = rest + rest * square * (-1.6666654611e-1 + square * (8.3321608736e-3 + square * -1.9515295891e-4))
    cosine = 1.0 + square * (-0.5 + square * (4.166664568298827e-2 + square * (-1.388731625493765e-3 + square * 2.443315711809948e-5)))
    odd = (quadrant & 1) == 1
    flip_sine = (quadrant & 2) == 2
    flip_cosine = ((quadrant + 1) & 2) == 2
    first = jnp.where(odd, cosine, sine)
    second = jnp.where(odd, sine, cosine)
    return jnp.where(flip_sine, -first, first), jnp.where(flip_cosine, -second, second)


def across(count, steps, load, store, table=None):
    def step(at, carry):
        row = pl.multiple_of(at * 8, 8)
        sign = sign_row()
        main = short_transform([Split(load(s, 0, row), load(s, 1, row)) for s in range(count)])
        for k in range(count):
            item = main[k]
            if table is not None:
                item = item.turn(*table(k, row, False))
            store(k, 0, row, item.real)
            store(k, 1, row, item.imag)
        tail = short_transform([Joint(load(s, 2, row), sign) for s in range(count)])
        for k in range(count):
            item = tail[k]
            value = item.both
            if table is not None:
                cosine, signed = table(k, row, True)
                value = value * cosine + swap(value) * signed
            store(k, 2, row, value)
        return carry

    lax.fori_loop(0, steps, step, 0)


def lane_lookup(table_ref):
    def look(k, row, tail):
        at = 2 if tail else 0
        return table_ref[k, at:at + 1, :], table_ref[k, at + 1:at + 2, :]

    return look


def column_lookup(table_ref, count):
    def look(k, row, tail):
        cosine = jnp.broadcast_to(table_ref[pl.ds(row, 8), k:k + 1], (8, LANES))
        sine = jnp.broadcast_to(table_ref[pl.ds(row, 8), count + k:count + k + 1], (8, LANES))
        return cosine, (sine * sign_row() if tail else sine)

    return look


def column_product(matrix_ref, value):
    high, low = halves(value)
    both = product(matrix_ref[0], matrix_ref[1], high, low, NORMAL)
    outs = both.shape[0] // 2
    first, second = both[:outs], both[outs:]
    sign = sign_row()[:1]
    real = first[:, :LANES] + second[:, LANES:2 * LANES]
    imag = first[:, LANES:2 * LANES] - second[:, :LANES]
    tail = first[:, 2 * LANES:] - swap(second[:, 2 * LANES:]) * sign
    return real, imag, tail


def flipped_product(matrix_ref, value):
    high, low = halves(value)
    both = product(matrix_ref[0], matrix_ref[1], high, low, FLIPPED)
    outs = both.shape[0] // 2
    width = both.shape[1] - LANES
    real, imag = both[:outs], both[outs:]
    pieces = [real[:, LANES:], imag[:, LANES:]]
    if width < LANES // 2:
        gap = jnp.zeros((outs, LANES // 2 - width), jnp.float32)
        pieces = [pieces[0], gap, pieces[1], gap]
    return real[:, :LANES], imag[:, :LANES], jnp.concatenate(pieces, axis=1)


def joined(ref, *lead):
    return jnp.concatenate([ref[lead + (plane,)] for plane in range(3)], axis=-1)


def column_turn(parts, cosine, sine):
    real, imag, tail = parts
    sign = sign_row()[:1]
    return (
        real * cosine - imag * sine,
        real * sine + imag * cosine,
        tail * cosine + swap(tail) * (sine * sign),
    )


def pick_column(table_ref, at, rows, count):
    lane = lax.broadcasted_iota(jnp.int32, (rows, 2 * count), 1)
    table = table_ref[...]
    cosine = jnp.sum(jnp.where(lane == at, table, 0.0), axis=1, keepdims=True)
    sine = jnp.sum(jnp.where(lane == at + count, table, 0.0), axis=1, keepdims=True)
    return jnp.broadcast_to(cosine, (rows, LANES)), jnp.broadcast_to(sine, (rows, LANES))


def whole(count):
    return [pl.BlockSpec(memory_space=pltpu.VMEM)] * count


def kernel_call(body, outs, inputs, scratch):
    return pl.pallas_call(
        body,
        out_shape=outs,
        in_specs=whole(len(inputs)),
        out_specs=jax.tree.map(lambda _: pl.BlockSpec(memory_space=pltpu.VMEM), outs),
        scratch_shapes=scratch,
        compiler_params=pltpu.CompilerParams(vmem_limit_bytes=62 * 1024 * 1024),
    )(*inputs)


class Plan:
    def __init__(self, length, row_count, col_count):
        self.length, self.row_count, self.col_count = length, row_count, col_count
        self.count = row_count * col_count
        self.each = length // self.count
        reach = length // 3 + 8
        near = -(-reach // self.count)
        near = (near + 3) // 4 * 4
        steps = np.arange(self.each)
        self.kept = np.concatenate([steps[:near], steps[self.each - near:]])
        self.keep = len(self.kept)
        self.near = near
        scale = 1.0 / math.sqrt(length)
        index = np.arange(self.each)
        self.full = phase_of(np.outer(index, index), self.each)
        self.cut = phase_of(np.outer(self.kept, index), self.each)
        self.scale = scale
        twist = 2.0 * np.pi * np.outer(np.arange(self.count), index) / length
        self.lane_twist = lane_table(twist)
        self.column_twist = column_table(twist.T)
        self.tall = rows_matrix(self.full, scale)
        self.tall_cut = rows_matrix(self.cut, scale)
        self.tall_back = rows_matrix(self.cut.T, scale)
        self.flip = transposed_matrix(self.full, scale)
        self.flip_cut = transposed_matrix(self.cut, scale)
        self.square = lane_square(self.cut, scale)
        far = np.arange(self.count)[:, None] + self.count * self.kept[None, :]
        self.far_chirp = lane_table(np.pi * (far * far % (2 * length)) / length)

    def slot(self, block):
        return block % self.row_count * self.col_count + block // self.row_count


def first_kernel(plan, x_ref, matrix_ref, twist_ref, out_ref, work_ref):
    count, each = plan.count, plan.each
    part = each // plan.row_count

    def step(s, carry):
        planes = [
            jnp.concatenate([x_ref[p, plane, pl.ds(s, part, stride=count), :] for p in range(plan.row_count)], axis=0)
            for plane in range(3)
        ]
        parts = column_product(matrix_ref, jnp.concatenate(planes, axis=-1))
        cosine, sine = pick_column(twist_ref, s, each, count)
        for plane, value in enumerate(column_turn(parts, cosine, sine)):
            work_ref[s, plane] = value
        return carry

    lax.fori_loop(0, count, step, 0)

    def load(s, plane, row):
        return work_ref[s, plane, pl.ds(row, 8), :]

    def store(k, plane, row, value):
        out_ref[k, plane, pl.ds(row, 8), :] = value

    across(count, each // 8, load, store)


def second_kernel(plan, x_ref, kerr_ref, theta_ref, own_ref, flip_ref, cut_ref, lane_ref, column_ref,
                  out_ref, phase_ref, work_ref, field_ref):
    count, each = plan.count, plan.each

    def load(s, plane, row):
        return x_ref[plan.slot(s), plane, pl.ds(row, 8), :]

    def store(k, plane, row, value):
        work_ref[k, plane, pl.ds(row, 8), :] = value

    across(count, each // 8, load, store, lane_lookup(lane_ref))

    def turn(k, carry):
        for plane, value in enumerate(flipped_product(flip_ref, joined(work_ref, k))):
            field_ref[plane, pl.ds(k, each, stride=count), :] = value
        return carry

    lax.fori_loop(0, count, turn, 0)
    size = 32

    def kerr(at, carry):
        rows = pl.ds(pl.multiple_of(at * size, size), size)
        sign = sign_row()[:1]
        theta = theta_ref[rows, :]
        real, imag, tail = field_ref[0, rows, :], field_ref[1, rows, :], field_ref[2, rows, :]
        phase = kerr_ref[0, rows, :] * (real * real + imag * imag)
        phase_ref[0, rows, :] = phase
        sine, cosine = sine_cosine(phase + (theta + own_ref[0:1, :]))
        field_ref[0, rows, :] = real * cosine - imag * sine
        field_ref[1, rows, :] = real * sine + imag * cosine
        square = tail * tail
        phase = kerr_ref[1, rows, :] * (square + swap(square))
        phase_ref[1, rows, :] = phase
        sine, cosine = sine_cosine(phase + (theta + own_ref[1:2, :]))
        field_ref[2, rows, :] = tail * cosine + swap(tail) * (sine * sign)
        return carry

    lax.fori_loop(0, plan.length // size, kerr, 0)

    def again(s, plane, row):
        return field_ref[plane, pl.ds(s * each + row, 8), :]

    across(count, each // 8, again, store, column_lookup(column_ref, count))

    def send(k, carry):
        for plane, value in enumerate(column_product(cut_ref, joined(work_ref, k))):
            out_ref[k, plane] = value
        return carry

    lax.fori_loop(0, count, send, 0)


def third_kernel(plan, x_ref, matrix_ref, lane_ref, out_ref, work_ref):
    def load(s, plane, row):
        return x_ref[s, plane, pl.ds(row, 8), :]

    def store(k, plane, row, value):
        work_ref[k, plane, pl.ds(row, 8), :] = value

    across(plan.count, plan.keep // 8, load, store, lane_lookup(lane_ref))

    def send(k, carry):
        for plane, value in enumerate(flipped_product(matrix_ref, joined(work_ref, k))):
            out_ref[k, plane] = value
        return carry

    lax.fori_loop(0, plan.count, send, 0)


def fourth_kernel(plan, x_ref, mask_ref, own_ref, chirp_ref, matrix_ref, lane_ref, out_ref, work_ref):
    def step(d, carry):
        sign = sign_row()[:1]
        own_cos, own_sin = own_ref[0], own_ref[1]
        main, tail_mask = mask_ref[d, 0], mask_ref[d, 1]
        far = chirp_ref[d]
        cosine = (own_cos * far[0:1] - own_sin * far[1:2]) * main
        sine = (own_cos * far[1:2] + own_sin * far[0:1]) * main
        real, imag, tail = x_ref[d, 0], x_ref[d, 1], x_ref[d, 2]
        own_tail = own_sin * sign
        tail = tail * (own_cos * tail_mask) + swap(tail) * (own_tail * tail_mask)
        tail = tail * far[2:3] + swap(tail) * far[3:4]
        value = jnp.concatenate([real * cosine - imag * sine, real * sine + imag * cosine, tail], axis=-1)
        high, low = halves(value)
        both = product(high, low, matrix_ref[0], matrix_ref[1], NORMAL)
        real, imag, tail = both[:, :LANES], both[:, LANES:2 * LANES], both[:, 2 * LANES:]
        twist = lane_ref[d]
        work_ref[d, 0] = real * twist[0:1] - imag * twist[1:2]
        work_ref[d, 1] = real * twist[1:2] + imag * twist[0:1]
        work_ref[d, 2] = tail * twist[2:3] + swap(tail) * twist[3:4]
        return carry

    lax.fori_loop(0, plan.count, step, 0)

    def load(s, plane, row):
        return work_ref[s, plane, pl.ds(row, 8), :]

    def store(k, plane, row, value):
        out_ref[plan.slot(k), plane, pl.ds(row, 8), :] = value

    across(plan.count, plan.keep // 8, load, store)


def fifth_kernel(plan, x_ref, matrix_ref, column_ref, out_ref, work_ref):
    def step(e, carry):
        parts = column_product(matrix_ref, joined(x_ref, e))
        cosine, sine = pick_column(column_ref, e, plan.each, plan.count)
        for plane, value in enumerate(column_turn(parts, cosine, sine)):
            work_ref[e, plane] = value
        return carry

    lax.fori_loop(0, plan.count, step, 0)

    def load(s, plane, row):
        return work_ref[s, plane, pl.ds(row, 8), :]

    def store(k, plane, row, value):
        out_ref[k, plane, pl.ds(row, 8), :] = value

    across(plan.count, plan.each // 8, load, store)


def f32(*shape):
    return jax.ShapeDtypeStruct(shape, jnp.float32)


def scratch(*shape):
    return pltpu.VMEM(shape, jnp.float32)


def square_angle(index, length):
    return (math.pi / length) * (index * index % (2 * length)).astype(jnp.float32)


def pack_kernel(plan, real_ref, imag_ref, kerr_ref, down_ref, along_ref, out_ref):
    size = 16
    pairs = plan.row_count // 2

    def step(at, carry):
        rows = pl.ds(pl.multiple_of(at * size, size), size)
        low = lax.broadcasted_iota(jnp.int32, (size, LANES), 1) < LANES // 2
        down = down_ref[rows, :]
        for pair in range(pairs):
            tiles = []
            for tile in range(3):
                lanes = slice((3 * pair + tile) * LANES, (3 * pair + tile + 1) * LANES)
                real, imag = real_ref[rows, lanes], imag_ref[rows, lanes]
                phase = kerr_ref[rows, lanes] * (real * real + imag * imag)
                sine, cosine = sine_cosine(phase + (down + along_ref[0:1, lanes]))
                tiles.append((real * cosine - imag * sine, real * sine + imag * cosine))
            (real_a, imag_a), (real_b, imag_b), (real_c, imag_c) = tiles
            even, odd = 2 * pair, 2 * pair + 1
            out_ref[even, 0, rows, :] = real_a
            out_ref[even, 1, rows, :] = imag_a
            out_ref[even, 2, rows, :] = jnp.where(low, real_b, swap(imag_b))
            turned = swap(real_c)
            out_ref[odd, 0, rows, :] = jnp.where(low, swap(real_b), turned)
            out_ref[odd, 1, rows, :] = jnp.where(low, swap(imag_b), swap(imag_c))
            out_ref[odd, 2, rows, :] = jnp.where(low, turned, imag_c)
        return carry

    lax.fori_loop(0, real_ref.shape[0] // size, step, 0)


def pack_field(plan, field_real, field_imag, kerr_map, down, along):
    rows_here, cols_here = field_real.shape
    rows = rows_here // plan.col_count
    tile = pl.BlockSpec((rows, cols_here), lambda i: (i, 0))
    return pl.pallas_call(
        functools.partial(pack_kernel, plan),
        out_shape=f32(plan.row_count, 3, rows_here, LANES),
        grid=(plan.col_count,),
        in_specs=[tile, tile, tile, pl.BlockSpec((rows, LANES), lambda i: (i, 0)), pl.BlockSpec((1, cols_here), lambda i: (0, 0))],
        out_specs=pl.BlockSpec((plan.row_count, 3, rows, LANES), lambda i: (0, 0, i, 0)),
        compiler_params=pltpu.CompilerParams(vmem_limit_bytes=40 * 1024 * 1024),
    )(field_real, field_imag, kerr_map, jnp.broadcast_to(down[:, None], (rows_here, LANES)), along[None, :])


def unpack_kernel(plan, field_ref, real_ref, imag_ref):
    size = 16

    def step(at, carry):
        rows = pl.ds(pl.multiple_of(at * size, size), size)
        low = lax.broadcasted_iota(jnp.int32, (size, LANES), 1) < LANES // 2
        for pair in range(plan.row_count // 2):
            even, odd = 2 * pair, 2 * pair + 1
            tails = field_ref[even, 0, 2, rows, :], field_ref[odd, 0, 2, rows, :]
            for plane, out_ref in enumerate((real_ref, imag_ref)):
                own = tails[0] if plane == 0 else swap(tails[0])
                last = swap(tails[1]) if plane == 0 else tails[1]
                turned = swap(field_ref[odd, 0, plane, rows, :])
                at_lane = 3 * pair * LANES
                out_ref[rows, at_lane:at_lane + LANES] = field_ref[even, 0, plane, rows, :]
                out_ref[rows, at_lane + LANES:at_lane + 2 * LANES] = jnp.where(low, own, turned)
                out_ref[rows, at_lane + 2 * LANES:at_lane + 3 * LANES] = jnp.where(low, turned, last)
        return carry

    lax.fori_loop(0, real_ref.shape[0] // size, step, 0)


def unpack_field(plan, field, rows_here, cols_here):
    tile = pl.BlockSpec((plan.each, cols_here), lambda i: (i, 0))
    return pl.pallas_call(
        functools.partial(unpack_kernel, plan),
        out_shape=(f32(rows_here, cols_here), f32(rows_here, cols_here)),
        grid=(plan.col_count,),
        in_specs=[pl.BlockSpec((plan.row_count, 1, 3, plan.each, LANES), lambda i: (0, i, 0, 0, 0))],
        out_specs=(tile, tile),
        compiler_params=pltpu.CompilerParams(vmem_limit_bytes=40 * 1024 * 1024),
    )(field)


def spread(plan, part, col_at):
    count = plan.col_count
    got = []
    for shift in range(count):
        block = lax.dynamic_index_in_dim(part, (col_at + shift) % count, 0, keepdims=True)
        if shift:
            block = lax.ppermute(block, "cols", [(z, (z + shift) % count) for z in range(count)])
        got.append(block)
    ring = got[::-1]
    return lax.dynamic_slice_in_dim(jnp.concatenate(ring + ring, axis=0), count - 1 - col_at, count, axis=0)


def fast_device(plan, field_real, field_imag, kerr_map, pinhole):
    length, count, each, keep = plan.length, plan.count, plan.each, plan.keep
    rows_here, cols_here = field_real.shape
    row_at, col_at = lax.axis_index("rows"), lax.axis_index("cols")
    own = row_at * plan.col_count + col_at
    both_axes = ("rows", "cols")
    index = jnp.arange(length, dtype=jnp.int32)
    theta = square_angle(index, length)

    phase_one = kerr_map * (field_real * field_real + field_imag * field_imag)
    down = lax.dynamic_slice(theta, (row_at * rows_here,), (rows_here,))
    along = lax.dynamic_slice(theta, (col_at * cols_here,), (cols_here,))
    packed_field = pack_field(plan, field_real, field_imag, kerr_map, down, along)
    field = lax.all_to_all(packed_field, "rows", split_axis=0, concat_axis=0, tiled=True)
    kerr = spread(plan, kerr_map.reshape(plan.col_count, each, cols_here), col_at)
    field, kerr = lax.optimization_barrier((field, kerr))
    kerr = jnp.transpose(kerr, (0, 2, 1)).reshape(length, each)
    kerr = jnp.stack([kerr[:, :LANES], jnp.concatenate([kerr[:, LANES:], kerr[:, LANES:]], axis=-1)])

    near = plan.near

    def cut(part, axis):
        size = part.shape[axis]
        return jnp.concatenate([
            lax.slice_in_dim(part, 0, near, axis=axis), lax.slice_in_dim(part, size - near, size, axis=axis)
        ], axis=axis)

    mask = jnp.transpose(cut(pinhole.reshape(each, count, each), 0), (1, 0, 2)).astype(jnp.float32)

    theta_wide = jnp.broadcast_to(theta[:, None] - math.pi / 2, (length, LANES))
    lines = lax.dynamic_slice(theta, (own * each,), (each,))
    own_theta = jnp.stack([lines[:LANES], jnp.concatenate([lines[LANES:], lines[LANES:]])])
    far = own + count * jnp.asarray(plan.kept, jnp.int32)
    far_angle = square_angle(far, length)
    own_chirp = jnp.broadcast_to(jnp.stack([jnp.cos(far_angle), -jnp.sin(far_angle)])[:, :, None], (2, keep, LANES))

    def exchange(part):
        return lax.all_to_all(part, both_axes, split_axis=0, concat_axis=0, tiled=True)

    field = kernel_call(
        functools.partial(first_kernel, plan), f32(count, 3, each, LANES),
        (field, plan.tall, plan.column_twist), [scratch(count, 3, each, LANES)],
    )
    field = exchange(field)
    field, mask = lax.optimization_barrier((field, mask))
    mask = lax.all_to_all(mask, both_axes, split_axis=0, concat_axis=0, tiled=True)
    field, phase_two = kernel_call(
        functools.partial(second_kernel, plan),
        (f32(count, 3, keep, LANES), f32(2, length, LANES)),
        (field, kerr, theta_wide, own_theta, plan.flip, plan.tall_cut, plan.lane_twist, plan.column_twist),
        [scratch(count, 3, each, LANES), scratch(3, length, LANES)],
    )
    field, mask = lax.optimization_barrier((field, mask))
    field = exchange(field)
    mask = jnp.transpose(mask, (1, 0, 2)).reshape(keep, each, count)
    mask = jnp.transpose(cut(mask, 1), (2, 0, 1))
    tail = jnp.pad(mask[..., LANES:], ((0, 0), (0, 0), (0, LANES // 2 - (keep - LANES))))
    mask = jnp.stack([mask[..., :LANES], jnp.concatenate([tail, tail], axis=-1)], axis=1)
    field = kernel_call(
        functools.partial(third_kernel, plan), f32(count, 3, keep, LANES),
        (field, plan.flip_cut, plan.lane_twist), [scratch(count, 3, keep, LANES)],
    )
    field = exchange(field)
    field = kernel_call(
        functools.partial(fourth_kernel, plan), f32(count, 3, keep, LANES),
        (field, mask, own_chirp, plan.far_chirp, plan.square, plan.lane_twist), [scratch(count, 3, keep, LANES)],
    )
    field = exchange(field)
    field = kernel_call(
        functools.partial(fifth_kernel, plan), f32(count, 3, each, LANES),
        (field, plan.tall_back, plan.column_twist), [scratch(count, 3, each, LANES)],
    )
    phase = jnp.concatenate([phase_two[0], phase_two[1][:, :LANES // 2]], axis=-1)
    phase = jnp.transpose(phase.reshape(plan.col_count, cols_here, each), (0, 2, 1))
    field, phase = lax.optimization_barrier((field, phase))
    field = field.reshape(plan.row_count, plan.col_count, 3, each, LANES)
    phase = spread(plan, phase, col_at)
    field = lax.all_to_all(field, "rows", split_axis=0, concat_axis=0, tiled=True)
    out_real, out_imag = unpack_field(plan, field, rows_here, cols_here)
    return (out_real, out_imag, phase_one + phase.reshape(rows_here, cols_here))


def suits(length, count):
    each = length // count
    return count == 32 and each - LANES == LANES // 2


def solution(mesh):
    placed = (P("rows", "cols"), P("rows", "cols"), P("rows", "cols"), P(None, ("rows", "cols")))

    def device(field_real, field_imag, kerr_map, pinhole):
        row_count, col_count = mesh.shape["rows"], mesh.shape["cols"]
        length = pinhole.shape[0]
        if suits(length, row_count * col_count):
            plan = Plan(length, row_count, col_count)
            return fast_device(plan, field_real, field_imag, kerr_map, pinhole)
        return per_device(field_real, field_imag, kerr_map, pinhole)

    return jax.shard_map(
        device,
        mesh=mesh,
        in_specs=placed,
        out_specs=(P("rows", "cols"), P("rows", "cols"), P("rows", "cols")),
        check_vma=False,
    )
```

```python
import functools
import math

import jax
import jax.numpy as jnp
import numpy as np
from jax import lax
from jax.experimental import pallas as pl
from jax.experimental.pallas import tpu as pltpu
from jax.sharding import PartitionSpec as P

RADIX = 128


def phase_pair(first, second, period):
    product = first[:, None] * second[None, :] % period
    angle = 2.0 * math.pi / period * product.astype(jnp.float32)
    return (jnp.cos(angle), jnp.sin(angle))


def complex_apply(form, real_part, imag_part, cos_table, sin_table, backward, precision):
    weight = 1.0 if backward else -1.0
    real_cos = jnp.einsum(form, real_part, cos_table, precision=precision)
    real_sin = jnp.einsum(form, real_part, sin_table, precision=precision)
    imag_cos = jnp.einsum(form, imag_part, cos_table, precision=precision)
    imag_sin = jnp.einsum(form, imag_part, sin_table, precision=precision)
    return (real_cos - weight * imag_sin, imag_cos + weight * real_sin)


def twiddle(real_part, imag_part, cos_table, sin_table, backward):
    weight = 1.0 if backward else -1.0
    return (
        real_part * cos_table - weight * imag_part * sin_table,
        imag_part * cos_table + weight * real_part * sin_table,
    )


def transform_last(real_part, imag_part, backward):
    rows_here, length = real_part.shape
    blocks = length // RADIX
    outer = jnp.arange(blocks, dtype=jnp.int32)
    inner = jnp.arange(RADIX, dtype=jnp.int32)
    real_part = real_part.reshape(rows_here, blocks, RADIX)
    imag_part = imag_part.reshape(rows_here, blocks, RADIX)
    cos_outer, sin_outer = phase_pair(outer, outer, blocks)
    real_part, imag_part = complex_apply(
        "mab,ak->mkb", real_part, imag_part, cos_outer, sin_outer, backward, lax.Precision.HIGH
    )
    cos_mid, sin_mid = phase_pair(outer, inner, length)
    real_part, imag_part = twiddle(real_part, imag_part, cos_mid, sin_mid, backward)
    cos_inner, sin_inner = phase_pair(inner, inner, RADIX)
    real_part, imag_part = complex_apply(
        "mkb,bj->mkj", real_part, imag_part, cos_inner, sin_inner, backward, lax.Precision.HIGH
    )
    scale = 1.0 / math.sqrt(length)
    real_part = jnp.transpose(real_part, (0, 2, 1)).reshape(rows_here, length) * scale
    imag_part = jnp.transpose(imag_part, (0, 2, 1)).reshape(rows_here, length) * scale
    return (real_part, imag_part)


def kerr_phase(real_part, imag_part, kerr_part):
    power = real_part * real_part + imag_part * imag_part
    phase = kerr_part * power
    cosine = jnp.cos(phase)
    sine = jnp.sin(phase)
    return (real_part * cosine - imag_part * sine, real_part * sine + imag_part * cosine, phase)


def to_tall(real_part, imag_part):
    rows_here, length = real_part.shape
    device_count = lax.axis_size(("rows", "cols"))
    each = length // device_count
    real_part = real_part.reshape(rows_here, device_count, each)
    imag_part = imag_part.reshape(rows_here, device_count, each)
    real_part, imag_part = (
        lax.all_to_all(real_part, ("rows", "cols"), split_axis=1, concat_axis=0, tiled=True),
        lax.all_to_all(imag_part, ("rows", "cols"), split_axis=1, concat_axis=0, tiled=True),
    )
    real_part = jnp.transpose(real_part.reshape(device_count, rows_here, each), (2, 0, 1))
    imag_part = jnp.transpose(imag_part.reshape(device_count, rows_here, each), (2, 0, 1))
    return (real_part.reshape(each, length), imag_part.reshape(each, length))


def from_tall(real_part, imag_part):
    each, length = real_part.shape
    device_count = lax.axis_size(("rows", "cols"))
    rows_here = length // device_count
    real_part = jnp.transpose(real_part.reshape(each, device_count, rows_here), (1, 2, 0))
    imag_part = jnp.transpose(imag_part.reshape(each, device_count, rows_here), (1, 2, 0))
    real_part, imag_part = (
        lax.all_to_all(real_part, ("rows", "cols"), split_axis=0, concat_axis=2, tiled=True),
        lax.all_to_all(imag_part, ("rows", "cols"), split_axis=0, concat_axis=2, tiled=True),
    )
    return (real_part.reshape(rows_here, length), imag_part.reshape(rows_here, length))


def chirp_line(index, length):
    square = index * index % (2 * length)
    angle = -(math.pi / length) * square.astype(jnp.float32)
    return (jnp.cos(angle), jnp.sin(angle))


def multiply(real_part, imag_part, other_real, other_imag):
    return (
        real_part * other_real - imag_part * other_imag,
        real_part * other_imag + imag_part * other_real,
    )


def spectral_pair(real_part, imag_part, table_real, table_imag, backward, precision):
    rows_here, length = real_part.shape
    blocks = length // RADIX
    outer = jnp.arange(blocks, dtype=jnp.int32)
    inner = jnp.arange(RADIX, dtype=jnp.int32)
    real_part = real_part.reshape(rows_here, blocks, RADIX)
    imag_part = imag_part.reshape(rows_here, blocks, RADIX)
    cos_outer, sin_outer = phase_pair(outer, outer, blocks)
    cos_mid, sin_mid = phase_pair(outer, inner, length)
    cos_inner, sin_inner = phase_pair(inner, inner, RADIX)
    real_part, imag_part = complex_apply(
        "mab,ak->mkb", real_part, imag_part, cos_outer, sin_outer, False, precision
    )
    real_part, imag_part = twiddle(real_part, imag_part, cos_mid, sin_mid, False)
    real_part, imag_part = complex_apply(
        "mkb,bj->mkj", real_part, imag_part, cos_inner, sin_inner, False, precision
    )
    real_part, imag_part = multiply(real_part, imag_part, table_real, table_imag)
    real_part, imag_part = complex_apply(
        "mkj,jb->mkb", real_part, imag_part, cos_inner, sin_inner, backward, precision
    )
    real_part, imag_part = twiddle(real_part, imag_part, cos_mid, sin_mid, backward)
    real_part, imag_part = complex_apply(
        "mkb,ka->mab", real_part, imag_part, cos_outer, sin_outer, backward, precision
    )
    return (real_part.reshape(rows_here, length), imag_part.reshape(rows_here, length))


def tile_to_columns(part):
    wide = lax.all_to_all(part, "rows", split_axis=1, concat_axis=0, tiled=True)
    return jnp.transpose(wide)


def columns_to_rows(real_part, imag_part):
    each, length = real_part.shape
    row_count, col_count = lax.axis_size("rows"), lax.axis_size("cols")
    device_count = row_count * col_count
    rows_here = length // device_count

    def send(part):
        part = part.reshape(each, row_count, col_count, rows_here)
        part = jnp.transpose(part, (2, 1, 3, 0)).reshape(device_count, rows_here, each)
        part = lax.all_to_all(part, ("cols", "rows"), split_axis=0, concat_axis=2, tiled=True)
        return part.reshape(rows_here, length)

    return (send(real_part), send(imag_part))


def per_device(field_real, field_imag, kerr_map, pinhole):
    real_part, imag_part, phase_one = kerr_phase(field_real, field_imag, kerr_map)
    real_part, imag_part = tile_to_columns(real_part), tile_to_columns(imag_part)
    kerr_wide = lax.all_to_all(kerr_map, "cols", split_axis=0, concat_axis=1, tiled=True)
    length, each = pinhole.shape
    blocks = length // RADIX
    scale = 1.0 / length
    split_index = (
        jnp.arange(blocks, dtype=jnp.int32)[:, None]
        + blocks * jnp.arange(RADIX, dtype=jnp.int32)[None, :]
    )
    line_cos, line_sin = chirp_line(split_index, length)
    line_cos, line_sin = line_cos * scale, line_sin * scale
    own = lax.axis_index(("rows", "cols")) * each + jnp.arange(each, dtype=jnp.int32)
    own_cos, own_sin = chirp_line(own, length)
    own_cos, own_sin = own_cos[:, None, None], own_sin[:, None, None]
    aperture = jnp.transpose(pinhole.reshape(RADIX, blocks, each), (2, 1, 0)).astype(jnp.float32)
    table_real, table_imag = multiply(line_cos[None], line_sin[None], own_cos, own_sin)
    table_real, table_imag = table_real * aperture, table_imag * aperture
    real_part, imag_part = spectral_pair(real_part, imag_part, line_cos, line_sin, True, lax.Precision.HIGHEST)
    real_part, imag_part = columns_to_rows(real_part, imag_part)
    real_part, imag_part = spectral_pair(real_part, imag_part, line_cos, line_sin, True, lax.Precision.HIGHEST)
    real_part, imag_part, phase_two = kerr_phase(real_part, imag_part, kerr_wide)
    phase_back = lax.all_to_all(phase_two, "cols", split_axis=1, concat_axis=0, tiled=True)
    real_part, imag_part = transform_last(real_part, imag_part, False)
    real_part, imag_part = to_tall(real_part, imag_part)
    real_part, imag_part = spectral_pair(real_part, imag_part, table_real, table_imag, False, lax.Precision.HIGH)
    real_part, imag_part = from_tall(real_part, imag_part)
    real_part, imag_part = transform_last(real_part, imag_part, False)
    out_real, out_imag = (
        lax.all_to_all(real_part, "cols", split_axis=1, concat_axis=0, tiled=True),
        lax.all_to_all(imag_part, "cols", split_axis=1, concat_axis=0, tiled=True),
    )
    return (out_real, out_imag, phase_one + phase_back)


LANES = 128


def as_pair(values):
    high = values.astype(np.float32).astype(jnp.bfloat16)
    low = (values - high.astype(np.float64)).astype(np.float32).astype(jnp.bfloat16)
    return np.stack([high, low])


def phase_of(product, period):
    return 2.0 * np.pi * (product % period) / period


def rows_matrix(angle, scale):
    return as_pair(np.concatenate([np.cos(angle), np.sin(angle)], axis=0) * scale)


def packed(values, tail_width=64):
    half = values.shape[-1] - LANES
    pad = [(0, 0)] * (values.ndim - 1) + [(0, tail_width - half)]
    return values[..., :LANES], np.pad(values[..., LANES:], pad)


def packed_columns(real_rows, imag_rows):
    real_main, real_tail = packed(real_rows)
    imag_main, imag_tail = packed(imag_rows)
    return np.concatenate([real_main, imag_main, real_tail, imag_tail], axis=-1)


def transposed_matrix(angle, scale):
    cosine, sine = np.cos(angle) * scale, np.sin(angle) * scale
    upper = packed_columns(cosine, sine)
    lower = packed_columns(-sine, cosine)
    return as_pair(np.concatenate([upper, lower], axis=0))


def lane_square(angle_in_out, scale):
    cosine, sine = np.cos(angle_in_out) * scale, np.sin(angle_in_out) * scale
    from_real = packed_columns(cosine, -sine)
    from_imag = packed_columns(sine, cosine)
    rows = from_real.shape[0]
    pad = np.zeros((64 - (rows - LANES), from_real.shape[1]))
    return as_pair(np.concatenate(
        [from_real[:LANES], from_imag[:LANES], from_real[LANES:], pad, from_imag[LANES:], pad], axis=0
    ))


def lane_table(angle):
    cosine, sine = np.cos(angle), -np.sin(angle)
    cos_main, cos_tail = packed(cosine)
    sin_main, sin_tail = packed(sine)
    return np.stack([
        cos_main, sin_main,
        np.concatenate([cos_tail, cos_tail], axis=-1),
        np.concatenate([-sin_tail, sin_tail], axis=-1),
    ], axis=1).astype(np.float32)


def column_table(angle):
    return np.concatenate([np.cos(angle), -np.sin(angle)], axis=1).astype(np.float32)


def sign_row():
    lane = lax.broadcasted_iota(jnp.int32, (8, LANES), 1)
    return jnp.where(lane < LANES // 2, -1.0, 1.0).astype(jnp.float32)


def swap(value):
    return pltpu.roll(value, LANES // 2, 1)


class Split:
    def __init__(self, real, imag):
        self.real, self.imag = real, imag

    def __add__(self, other):
        return Split(self.real + other.real, self.imag + other.imag)

    def __sub__(self, other):
        return Split(self.real - other.real, self.imag - other.imag)

    def turn(self, cosine, sine):
        return Split(self.real * cosine - self.imag * sine, self.real * sine + self.imag * cosine)

    def quarter(self):
        return Split(self.imag, -self.real)

    def eighth(self, half):
        return Split((self.real + self.imag) * half, (self.imag - self.real) * half)


class Joint:
    def __init__(self, both, sign):
        self.both, self.sign = both, sign

    def __add__(self, other):
        return Joint(self.both + other.both, self.sign)

    def __sub__(self, other):
        return Joint(self.both - other.both, self.sign)

    def turn(self, cosine, sine):
        return Joint(self.both * cosine + swap(self.both) * (self.sign * sine), self.sign)

    def quarter(self):
        return Joint(swap(self.both) * -self.sign, self.sign)

    def eighth(self, half):
        return self.turn(half, -half)


def short_transform(items):
    count = len(items)
    if count == 1:
        return items
    if count % 4:
        return [items[0] + items[1], items[0] - items[1]]
    quarter = count // 4
    parts = [short_transform(items[index::4]) for index in range(4)]
    out = [None] * count
    for index in range(quarter):
        turned = [parts[0][index]]
        for step in range(1, 4):
            place = step * index
            item = parts[step][index]
            if place == 0:
                turned.append(item)
            elif place * 8 == count:
                turned.append(item.eighth(math.sqrt(0.5)))
            elif place * 4 == count:
                turned.append(item.quarter())
            else:
                angle = -2.0 * math.pi * place / count
                turned.append(item.turn(math.cos(angle), math.sin(angle)))
        first, second, third, fourth = turned
        even, odd = first + third, first - third
        even_two, odd_two = second + fourth, (second - fourth).quarter()
        out[index] = even + even_two
        out[index + quarter] = odd + odd_two
        out[index + 2 * quarter] = even - even_two
        out[index + 3 * quarter] = odd - odd_two
    return out


def halves(value):
    high = value.astype(jnp.bfloat16)
    return high, (value - high.astype(jnp.float32)).astype(jnp.bfloat16)


def product(left_high, left_low, right_high, right_low, dims):
    def one(left, right):
        return lax.dot_general(left, right, (dims, ((), ())), preferred_element_type=jnp.float32)

    return one(left_high, right_high) + one(left_low, right_high) + one(left_high, right_low)


NORMAL = ((1,), (0,))
FLIPPED = ((1,), (1,))


def sine_cosine(angle):
    turns = jnp.floor(angle * (2.0 / math.pi) + 0.5)
    rest = angle - turns * 1.5703125
    rest = rest - turns * 4.837512969970703125e-4
    rest = rest - turns * 7.54978995489188216e-8
    quadrant = turns.astype(jnp.int32)
    square = rest * rest
    sine = rest + rest * square * (-1.6666654611e-1 + square * (8.3321608736e-3 + square * -1.9515295891e-4))
    cosine = 1.0 + square * (-0.5 + square * (4.166664568298827e-2 + square * (-1.388731625493765e-3 + square * 2.443315711809948e-5)))
    odd = (quadrant & 1) == 1
    flip_sine = (quadrant & 2) == 2
    flip_cosine = ((quadrant + 1) & 2) == 2
    first = jnp.where(odd, cosine, sine)
    second = jnp.where(odd, sine, cosine)
    return jnp.where(flip_sine, -first, first), jnp.where(flip_cosine, -second, second)


def across(count, steps, load, store, table=None):
    def step(at, carry):
        row = pl.multiple_of(at * 8, 8)
        sign = sign_row()
        main = short_transform([Split(load(s, 0, row), load(s, 1, row)) for s in range(count)])
        for k in range(count):
            item = main[k]
            if table is not None:
                item = item.turn(*table(k, row, False))
            store(k, 0, row, item.real)
            store(k, 1, row, item.imag)
        tail = short_transform([Joint(load(s, 2, row), sign) for s in range(count)])
        for k in range(count):
            item = tail[k]
            value = item.both
            if table is not None:
                cosine, signed = table(k, row, True)
                value = value * cosine + swap(value) * signed
            store(k, 2, row, value)
        return carry

    lax.fori_loop(0, steps, step, 0)


def lane_lookup(table_ref):
    def look(k, row, tail):
        at = 2 if tail else 0
        return table_ref[k, at:at + 1, :], table_ref[k, at + 1:at + 2, :]

    return look


def column_lookup(table_ref, count):
    def look(k, row, tail):
        cosine = jnp.broadcast_to(table_ref[pl.ds(row, 8), k:k + 1], (8, LANES))
        sine = jnp.broadcast_to(table_ref[pl.ds(row, 8), count + k:count + k + 1], (8, LANES))
        return cosine, (sine * sign_row() if tail else sine)

    return look


def column_product(matrix_ref, value):
    high, low = halves(value)
    both = product(matrix_ref[0], matrix_ref[1], high, low, NORMAL)
    outs = both.shape[0] // 2
    first, second = both[:outs], both[outs:]
    sign = sign_row()[:1]
    real = first[:, :LANES] + second[:, LANES:2 * LANES]
    imag = first[:, LANES:2 * LANES] - second[:, :LANES]
    tail = first[:, 2 * LANES:] - swap(second[:, 2 * LANES:]) * sign
    return real, imag, tail


def flipped_product(matrix_ref, value):
    high, low = halves(value)
    both = product(matrix_ref[0], matrix_ref[1], high, low, FLIPPED)
    outs = both.shape[0] // 2
    width = both.shape[1] - LANES
    real, imag = both[:outs], both[outs:]
    pieces = [real[:, LANES:], imag[:, LANES:]]
    if width < LANES // 2:
        gap = jnp.zeros((outs, LANES // 2 - width), jnp.float32)
        pieces = [pieces[0], gap, pieces[1], gap]
    return real[:, :LANES], imag[:, :LANES], jnp.concatenate(pieces, axis=1)


def joined(ref, *lead):
    return jnp.concatenate([ref[lead + (plane,)] for plane in range(3)], axis=-1)


def column_turn(parts, cosine, sine):
    real, imag, tail = parts
    sign = sign_row()[:1]
    return (
        real * cosine - imag * sine,
        real * sine + imag * cosine,
        tail * cosine + swap(tail) * (sine * sign),
    )


def pick_column(table_ref, at, rows, count):
    lane = lax.broadcasted_iota(jnp.int32, (rows, 2 * count), 1)
    table = table_ref[...]
    cosine = jnp.sum(jnp.where(lane == at, table, 0.0), axis=1, keepdims=True)
    sine = jnp.sum(jnp.where(lane == at + count, table, 0.0), axis=1, keepdims=True)
    return jnp.broadcast_to(cosine, (rows, LANES)), jnp.broadcast_to(sine, (rows, LANES))


def whole(count):
    return [pl.BlockSpec(memory_space=pltpu.VMEM)] * count


def kernel_call(body, outs, inputs, scratch):
    return pl.pallas_call(
        body,
        out_shape=outs,
        in_specs=whole(len(inputs)),
        out_specs=jax.tree.map(lambda _: pl.BlockSpec(memory_space=pltpu.VMEM), outs),
        scratch_shapes=scratch,
        compiler_params=pltpu.CompilerParams(vmem_limit_bytes=62 * 1024 * 1024),
    )(*inputs)


class Plan:
    def __init__(self, length, row_count, col_count):
        self.length, self.row_count, self.col_count = length, row_count, col_count
        self.count = row_count * col_count
        self.each = length // self.count
        reach = length // 3 + 8
        near = -(-reach // self.count)
        near = (near + 3) // 4 * 4
        steps = np.arange(self.each)
        self.kept = np.concatenate([steps[:near], steps[self.each - near:]])
        self.keep = len(self.kept)
        self.near = near
        scale = 1.0 / math.sqrt(length)
        index = np.arange(self.each)
        self.full = phase_of(np.outer(index, index), self.each)
        self.cut = phase_of(np.outer(self.kept, index), self.each)
        self.scale = scale
        twist = 2.0 * np.pi * np.outer(np.arange(self.count), index) / length
        self.lane_twist = lane_table(twist)
        self.column_twist = column_table(twist.T)
        self.tall = rows_matrix(self.full, scale)
        self.tall_cut = rows_matrix(self.cut, scale)
        self.tall_back = rows_matrix(self.cut.T, scale)
        self.flip = transposed_matrix(self.full, scale)
        self.flip_cut = transposed_matrix(self.cut, scale)
        self.square = lane_square(self.cut, scale)
        far = np.arange(self.count)[:, None] + self.count * self.kept[None, :]
        self.far_chirp = lane_table(np.pi * (far * far % (2 * length)) / length)

    def slot(self, block):
        return block % self.row_count * self.col_count + block // self.row_count


def first_kernel(plan, x_ref, matrix_ref, twist_ref, out_ref, work_ref):
    count, each = plan.count, plan.each
    part = each // plan.row_count

    def step(s, carry):
        planes = [
            jnp.concatenate([x_ref[p, plane, pl.ds(s, part, stride=count), :] for p in range(plan.row_count)], axis=0)
            for plane in range(3)
        ]
        parts = column_product(matrix_ref, jnp.concatenate(planes, axis=-1))
        cosine, sine = pick_column(twist_ref, s, each, count)
        for plane, value in enumerate(column_turn(parts, cosine, sine)):
            work_ref[s, plane] = value
        return carry

    lax.fori_loop(0, count, step, 0)

    def load(s, plane, row):
        return work_ref[s, plane, pl.ds(row, 8), :]

    def store(k, plane, row, value):
        out_ref[k, plane, pl.ds(row, 8), :] = value

    across(count, each // 8, load, store)


def second_kernel(plan, x_ref, kerr_ref, theta_ref, own_ref, flip_ref, cut_ref, lane_ref, column_ref,
                  out_ref, phase_ref, work_ref, field_ref):
    count, each = plan.count, plan.each

    def load(s, plane, row):
        return x_ref[plan.slot(s), plane, pl.ds(row, 8), :]

    def store(k, plane, row, value):
        work_ref[k, plane, pl.ds(row, 8), :] = value

    across(count, each // 8, load, store, lane_lookup(lane_ref))

    def turn(k, carry):
        for plane, value in enumerate(flipped_product(flip_ref, joined(work_ref, k))):
            field_ref[plane, pl.ds(k, each, stride=count), :] = value
        return carry

    lax.fori_loop(0, count, turn, 0)
    size = 32

    def kerr(at, carry):
        rows = pl.ds(pl.multiple_of(at * size, size), size)
        sign = sign_row()[:1]
        theta = theta_ref[rows, :]
        real, imag, tail = field_ref[0, rows, :], field_ref[1, rows, :], field_ref[2, rows, :]
        phase = kerr_ref[0, rows, :] * (real * real + imag * imag)
        phase_ref[0, rows, :] = phase
        sine, cosine = sine_cosine(phase + (theta + own_ref[0:1, :]))
        field_ref[0, rows, :] = real * cosine - imag * sine
        field_ref[1, rows, :] = real * sine + imag * cosine
        square = tail * tail
        phase = kerr_ref[1, rows, :] * (square + swap(square))
        phase_ref[1, rows, :] = phase
        sine, cosine = sine_cosine(phase + (theta + own_ref[1:2, :]))
        field_ref[2, rows, :] = tail * cosine + swap(tail) * (sine * sign)
        return carry

    lax.fori_loop(0, plan.length // size, kerr, 0)

    def again(s, plane, row):
        return field_ref[plane, pl.ds(s * each + row, 8), :]

    across(count, each // 8, again, store, column_lookup(column_ref, count))

    def send(k, carry):
        for plane, value in enumerate(column_product(cut_ref, joined(work_ref, k))):
            out_ref[k, plane] = value
        return carry

    lax.fori_loop(0, count, send, 0)


def third_kernel(plan, x_ref, matrix_ref, lane_ref, out_ref, work_ref):
    def load(s, plane, row):
        return x_ref[s, plane, pl.ds(row, 8), :]

    def store(k, plane, row, value):
        work_ref[k, plane, pl.ds(row, 8), :] = value

    across(plan.count, plan.keep // 8, load, store, lane_lookup(lane_ref))

    keep, extra = plan.keep, plan.keep - LANES

    def send(k, carry):
        value = joined(work_ref, k)
        high, low = halves(value[:LANES])
        both = product(matrix_ref[0], matrix_ref[1], high, low, FLIPPED)
        out_ref[k, 0:2 * keep, :] = both
        rest = jnp.concatenate([value[LANES:], jnp.zeros((16 - extra, value.shape[1]), jnp.float32)], axis=0)
        high, low = halves(rest)
        gap = jnp.zeros((extra, LANES - extra), jnp.float32)
        for part in range(2):
            rows = slice(part * keep, (part + 1) * keep)
            tail = product(high, low, matrix_ref[0, rows, :], matrix_ref[1, rows, :], FLIPPED)[:extra]
            at = 2 * keep + 2 * part * extra
            out_ref[k, at:at + extra, :] = tail[:, :LANES]
            out_ref[k, at + extra:at + 2 * extra, :] = jnp.concatenate([tail[:, LANES:], gap], axis=1)
        return carry

    lax.fori_loop(0, plan.count, send, 0)


def fourth_kernel(plan, x_ref, mask_ref, own_ref, chirp_ref, matrix_ref, lane_ref, out_ref, work_ref):
    def step(d, carry):
        sign = sign_row()[:1]
        own_cos, own_sin = own_ref[0], own_ref[1]
        main, tail_mask = mask_ref[d, 0], mask_ref[d, 1]
        far = chirp_ref[d]
        cosine = (own_cos * far[0:1] - own_sin * far[1:2]) * main
        sine = (own_cos * far[1:2] + own_sin * far[0:1]) * main
        keep, extra = plan.keep, plan.keep - LANES
        real, imag = x_ref[d, 0:keep, :], x_ref[d, keep:2 * keep, :]
        gap = jnp.zeros((LANES // 2 - extra, 2 * LANES), jnp.float32)
        pieces = []
        for part in range(2):
            at = 2 * keep + 2 * part * extra
            pieces.append(jnp.concatenate([x_ref[d, at:at + extra, :], x_ref[d, at + extra:at + 2 * extra, :]], axis=1))
            pieces.append(gap)
        tail = jnp.transpose(jnp.concatenate(pieces, axis=0))[:keep]
        own_tail = own_sin * sign
        tail = tail * (own_cos * tail_mask) + swap(tail) * (own_tail * tail_mask)
        tail = tail * far[2:3] + swap(tail) * far[3:4]
        value = jnp.concatenate([real * cosine - imag * sine, real * sine + imag * cosine, tail], axis=-1)
        high, low = halves(value)
        both = product(high, low, matrix_ref[0], matrix_ref[1], NORMAL)
        real, imag, tail = both[:, :LANES], both[:, LANES:2 * LANES], both[:, 2 * LANES:]
        twist = lane_ref[d]
        work_ref[d, 0] = real * twist[0:1] - imag * twist[1:2]
        work_ref[d, 1] = real * twist[1:2] + imag * twist[0:1]
        work_ref[d, 2] = tail * twist[2:3] + swap(tail) * twist[3:4]
        return carry

    lax.fori_loop(0, plan.count, step, 0)

    def load(s, plane, row):
        return work_ref[s, plane, pl.ds(row, 8), :]

    def store(k, plane, row, value):
        out_ref[plan.slot(k), plane, pl.ds(row, 8), :] = value

    across(plan.count, plan.keep // 8, load, store)


def fifth_kernel(plan, x_ref, matrix_ref, column_ref, out_ref, work_ref):
    def step(e, carry):
        parts = column_product(matrix_ref, joined(x_ref, e))
        cosine, sine = pick_column(column_ref, e, plan.each, plan.count)
        for plane, value in enumerate(column_turn(parts, cosine, sine)):
            work_ref[e, plane] = value
        return carry

    lax.fori_loop(0, plan.count, step, 0)

    def load(s, plane, row):
        return work_ref[s, plane, pl.ds(row, 8), :]

    def store(k, plane, row, value):
        out_ref[k, plane, pl.ds(row, 8), :] = value

    across(plan.count, plan.each // 8, load, store)


def f32(*shape):
    return jax.ShapeDtypeStruct(shape, jnp.float32)


def scratch(*shape):
    return pltpu.VMEM(shape, jnp.float32)


def square_angle(index, length):
    return (math.pi / length) * (index * index % (2 * length)).astype(jnp.float32)


def pack_kernel(plan, real_ref, imag_ref, kerr_ref, down_ref, along_ref, out_ref):
    size = 16
    pairs = plan.row_count // 2

    def step(at, carry):
        rows = pl.ds(pl.multiple_of(at * size, size), size)
        low = lax.broadcasted_iota(jnp.int32, (size, LANES), 1) < LANES // 2
        down = down_ref[rows, :]
        for pair in range(pairs):
            tiles = []
            for tile in range(3):
                lanes = slice((3 * pair + tile) * LANES, (3 * pair + tile + 1) * LANES)
                real, imag = real_ref[rows, lanes], imag_ref[rows, lanes]
                phase = kerr_ref[rows, lanes] * (real * real + imag * imag)
                sine, cosine = sine_cosine(phase + (down + along_ref[0:1, lanes]))
                tiles.append((real * cosine - imag * sine, real * sine + imag * cosine))
            (real_a, imag_a), (real_b, imag_b), (real_c, imag_c) = tiles
            even, odd = 2 * pair, 2 * pair + 1
            out_ref[even, 0, rows, :] = real_a
            out_ref[even, 1, rows, :] = imag_a
            out_ref[even, 2, rows, :] = jnp.where(low, real_b, swap(imag_b))
            turned = swap(real_c)
            out_ref[odd, 0, rows, :] = jnp.where(low, swap(real_b), turned)
            out_ref[odd, 1, rows, :] = jnp.where(low, swap(imag_b), swap(imag_c))
            out_ref[odd, 2, rows, :] = jnp.where(low, turned, imag_c)
        return carry

    lax.fori_loop(0, real_ref.shape[0] // size, step, 0)


def pack_field(plan, field_real, field_imag, kerr_map, down, along):
    rows_here, cols_here = field_real.shape
    rows = rows_here // plan.col_count
    tile = pl.BlockSpec((rows, cols_here), lambda i: (i, 0))
    return pl.pallas_call(
        functools.partial(pack_kernel, plan),
        out_shape=f32(plan.row_count, 3, rows_here, LANES),
        grid=(plan.col_count,),
        in_specs=[tile, tile, tile, pl.BlockSpec((rows, LANES), lambda i: (i, 0)), pl.BlockSpec((1, cols_here), lambda i: (0, 0))],
        out_specs=pl.BlockSpec((plan.row_count, 3, rows, LANES), lambda i: (0, 0, i, 0)),
        compiler_params=pltpu.CompilerParams(vmem_limit_bytes=40 * 1024 * 1024),
    )(field_real, field_imag, kerr_map, jnp.broadcast_to(down[:, None], (rows_here, LANES)), along[None, :])


def unpack_kernel(plan, field_ref, real_ref, imag_ref):
    size = 16

    def step(at, carry):
        rows = pl.ds(pl.multiple_of(at * size, size), size)
        low = lax.broadcasted_iota(jnp.int32, (size, LANES), 1) < LANES // 2
        for pair in range(plan.row_count // 2):
            even, odd = 2 * pair, 2 * pair + 1
            tails = field_ref[even, 0, 2, rows, :], field_ref[odd, 0, 2, rows, :]
            for plane, out_ref in enumerate((real_ref, imag_ref)):
                own = tails[0] if plane == 0 else swap(tails[0])
                last = swap(tails[1]) if plane == 0 else tails[1]
                turned = swap(field_ref[odd, 0, plane, rows, :])
                at_lane = 3 * pair * LANES
                out_ref[rows, at_lane:at_lane + LANES] = field_ref[even, 0, plane, rows, :]
                out_ref[rows, at_lane + LANES:at_lane + 2 * LANES] = jnp.where(low, own, turned)
                out_ref[rows, at_lane + 2 * LANES:at_lane + 3 * LANES] = jnp.where(low, turned, last)
        return carry

    lax.fori_loop(0, real_ref.shape[0] // size, step, 0)


def unpack_field(plan, field, rows_here, cols_here):
    tile = pl.BlockSpec((plan.each, cols_here), lambda i: (i, 0))
    return pl.pallas_call(
        functools.partial(unpack_kernel, plan),
        out_shape=(f32(rows_here, cols_here), f32(rows_here, cols_here)),
        grid=(plan.col_count,),
        in_specs=[pl.BlockSpec((plan.row_count, 1, 3, plan.each, LANES), lambda i: (0, i, 0, 0, 0))],
        out_specs=(tile, tile),
        compiler_params=pltpu.CompilerParams(vmem_limit_bytes=40 * 1024 * 1024),
    )(field)


def spread(plan, part, col_at):
    count = plan.col_count
    got = []
    for shift in range(count):
        block = lax.dynamic_index_in_dim(part, (col_at + shift) % count, 0, keepdims=True)
        if shift:
            block = lax.ppermute(block, "cols", [(z, (z + shift) % count) for z in range(count)])
        got.append(block)
    ring = got[::-1]
    return lax.dynamic_slice_in_dim(jnp.concatenate(ring + ring, axis=0), count - 1 - col_at, count, axis=0)


def fast_device(plan, field_real, field_imag, kerr_map, pinhole):
    length, count, each, keep = plan.length, plan.count, plan.each, plan.keep
    rows_here, cols_here = field_real.shape
    row_at, col_at = lax.axis_index("rows"), lax.axis_index("cols")
    own = row_at * plan.col_count + col_at
    both_axes = ("rows", "cols")
    index = jnp.arange(length, dtype=jnp.int32)
    theta = square_angle(index, length)

    phase_one = kerr_map * (field_real * field_real + field_imag * field_imag)
    down = lax.dynamic_slice(theta, (row_at * rows_here,), (rows_here,))
    along = lax.dynamic_slice(theta, (col_at * cols_here,), (cols_here,))
    packed_field = pack_field(plan, field_real, field_imag, kerr_map, down, along)
    field = lax.all_to_all(packed_field, "rows", split_axis=0, concat_axis=0, tiled=True)
    kerr = spread(plan, kerr_map.reshape(plan.col_count, each, cols_here), col_at)
    field, kerr = lax.optimization_barrier((field, kerr))
    kerr = jnp.transpose(kerr, (0, 2, 1)).reshape(length, each)
    kerr = jnp.stack([kerr[:, :LANES], jnp.concatenate([kerr[:, LANES:], kerr[:, LANES:]], axis=-1)])

    near = plan.near

    def cut(part, axis):
        size = part.shape[axis]
        return jnp.concatenate([
            lax.slice_in_dim(part, 0, near, axis=axis), lax.slice_in_dim(part, size - near, size, axis=axis)
        ], axis=axis)

    mask = jnp.transpose(cut(pinhole.reshape(each, count, each), 0), (1, 0, 2)).astype(jnp.float32)

    theta_wide = jnp.broadcast_to(theta[:, None] - math.pi / 2, (length, LANES))
    lines = lax.dynamic_slice(theta, (own * each,), (each,))
    own_theta = jnp.stack([lines[:LANES], jnp.concatenate([lines[LANES:], lines[LANES:]])])
    far = own + count * jnp.asarray(plan.kept, jnp.int32)
    far_angle = square_angle(far, length)
    own_chirp = jnp.broadcast_to(jnp.stack([jnp.cos(far_angle), -jnp.sin(far_angle)])[:, :, None], (2, keep, LANES))

    def exchange(part):
        return lax.all_to_all(part, both_axes, split_axis=0, concat_axis=0, tiled=True)

    field = kernel_call(
        functools.partial(first_kernel, plan), f32(count, 3, each, LANES),
        (field, plan.tall, plan.column_twist), [scratch(count, 3, each, LANES)],
    )
    field = exchange(field)
    field, mask = lax.optimization_barrier((field, mask))
    mask = lax.all_to_all(mask, both_axes, split_axis=0, concat_axis=0, tiled=True)
    field, phase_two = kernel_call(
        functools.partial(second_kernel, plan),
        (f32(count, 3, keep, LANES), f32(2, length, LANES)),
        (field, kerr, theta_wide, own_theta, plan.flip, plan.tall_cut, plan.lane_twist, plan.column_twist),
        [scratch(count, 3, each, LANES), scratch(3, length, LANES)],
    )
    field, mask = lax.optimization_barrier((field, mask))
    field = exchange(field)
    mask = jnp.transpose(mask, (1, 0, 2)).reshape(keep, each, count)
    mask = jnp.transpose(cut(mask, 1), (2, 0, 1))
    tail = jnp.pad(mask[..., LANES:], ((0, 0), (0, 0), (0, LANES // 2 - (keep - LANES))))
    mask = jnp.stack([mask[..., :LANES], jnp.concatenate([tail, tail], axis=-1)], axis=1)
    field = kernel_call(
        functools.partial(third_kernel, plan), f32(count, 2 * keep + 4 * (keep - LANES), LANES),
        (field, plan.flip_cut, plan.lane_twist), [scratch(count, 3, keep, LANES)],
    )
    field = exchange(field)
    field = kernel_call(
        functools.partial(fourth_kernel, plan), f32(count, 3, keep, LANES),
        (field, mask, own_chirp, plan.far_chirp, plan.square, plan.lane_twist), [scratch(count, 3, keep, LANES)],
    )
    field = exchange(field)
    field = kernel_call(
        functools.partial(fifth_kernel, plan), f32(count, 3, each, LANES),
        (field, plan.tall_back, plan.column_twist), [scratch(count, 3, each, LANES)],
    )
    phase = jnp.concatenate([phase_two[0], phase_two[1][:, :LANES // 2]], axis=-1)
    phase = jnp.transpose(phase.reshape(plan.col_count, cols_here, each), (0, 2, 1))
    field, phase = lax.optimization_barrier((field, phase))
    field = field.reshape(plan.row_count, plan.col_count, 3, each, LANES)
    phase = spread(plan, phase, col_at)
    field = lax.all_to_all(field, "rows", split_axis=0, concat_axis=0, tiled=True)
    out_real, out_imag = unpack_field(plan, field, rows_here, cols_here)
    return (out_real, out_imag, phase_one + phase.reshape(rows_here, cols_here))


def suits(length, count):
    each = length // count
    return count == 32 and each - LANES == LANES // 2


def solution(mesh):
    placed = (P("rows", "cols"), P("rows", "cols"), P("rows", "cols"), P(None, ("rows", "cols")))

    def device(field_real, field_imag, kerr_map, pinhole):
        row_count, col_count = mesh.shape["rows"], mesh.shape["cols"]
        length = pinhole.shape[0]
        if suits(length, row_count * col_count):
            plan = Plan(length, row_count, col_count)
            return fast_device(plan, field_real, field_imag, kerr_map, pinhole)
        return per_device(field_real, field_imag, kerr_map, pinhole)

    return jax.shard_map(
        device,
        mesh=mesh,
        in_specs=placed,
        out_specs=(P("rows", "cols"), P("rows", "cols"), P("rows", "cols")),
        check_vma=False,
    )
```

```python
import functools
import math

import jax
import jax.numpy as jnp
import numpy as np
from jax import lax
from jax.experimental import pallas as pl
from jax.experimental.pallas import tpu as pltpu
from jax.sharding import PartitionSpec as P

RADIX = 128


def phase_pair(first, second, period):
    product = first[:, None] * second[None, :] % period
    angle = 2.0 * math.pi / period * product.astype(jnp.float32)
    return (jnp.cos(angle), jnp.sin(angle))


def complex_apply(form, real_part, imag_part, cos_table, sin_table, backward, precision):
    weight = 1.0 if backward else -1.0
    real_cos = jnp.einsum(form, real_part, cos_table, precision=precision)
    real_sin = jnp.einsum(form, real_part, sin_table, precision=precision)
    imag_cos = jnp.einsum(form, imag_part, cos_table, precision=precision)
    imag_sin = jnp.einsum(form, imag_part, sin_table, precision=precision)
    return (real_cos - weight * imag_sin, imag_cos + weight * real_sin)


def twiddle(real_part, imag_part, cos_table, sin_table, backward):
    weight = 1.0 if backward else -1.0
    return (
        real_part * cos_table - weight * imag_part * sin_table,
        imag_part * cos_table + weight * real_part * sin_table,
    )


def transform_last(real_part, imag_part, backward):
    rows_here, length = real_part.shape
    blocks = length // RADIX
    outer = jnp.arange(blocks, dtype=jnp.int32)
    inner = jnp.arange(RADIX, dtype=jnp.int32)
    real_part = real_part.reshape(rows_here, blocks, RADIX)
    imag_part = imag_part.reshape(rows_here, blocks, RADIX)
    cos_outer, sin_outer = phase_pair(outer, outer, blocks)
    real_part, imag_part = complex_apply(
        "mab,ak->mkb", real_part, imag_part, cos_outer, sin_outer, backward, lax.Precision.HIGH
    )
    cos_mid, sin_mid = phase_pair(outer, inner, length)
    real_part, imag_part = twiddle(real_part, imag_part, cos_mid, sin_mid, backward)
    cos_inner, sin_inner = phase_pair(inner, inner, RADIX)
    real_part, imag_part = complex_apply(
        "mkb,bj->mkj", real_part, imag_part, cos_inner, sin_inner, backward, lax.Precision.HIGH
    )
    scale = 1.0 / math.sqrt(length)
    real_part = jnp.transpose(real_part, (0, 2, 1)).reshape(rows_here, length) * scale
    imag_part = jnp.transpose(imag_part, (0, 2, 1)).reshape(rows_here, length) * scale
    return (real_part, imag_part)


def kerr_phase(real_part, imag_part, kerr_part):
    power = real_part * real_part + imag_part * imag_part
    phase = kerr_part * power
    cosine = jnp.cos(phase)
    sine = jnp.sin(phase)
    return (real_part * cosine - imag_part * sine, real_part * sine + imag_part * cosine, phase)


def to_tall(real_part, imag_part):
    rows_here, length = real_part.shape
    device_count = lax.axis_size(("rows", "cols"))
    each = length // device_count
    real_part = real_part.reshape(rows_here, device_count, each)
    imag_part = imag_part.reshape(rows_here, device_count, each)
    real_part, imag_part = (
        lax.all_to_all(real_part, ("rows", "cols"), split_axis=1, concat_axis=0, tiled=True),
        lax.all_to_all(imag_part, ("rows", "cols"), split_axis=1, concat_axis=0, tiled=True),
    )
    real_part = jnp.transpose(real_part.reshape(device_count, rows_here, each), (2, 0, 1))
    imag_part = jnp.transpose(imag_part.reshape(device_count, rows_here, each), (2, 0, 1))
    return (real_part.reshape(each, length), imag_part.reshape(each, length))


def from_tall(real_part, imag_part):
    each, length = real_part.shape
    device_count = lax.axis_size(("rows", "cols"))
    rows_here = length // device_count
    real_part = jnp.transpose(real_part.reshape(each, device_count, rows_here), (1, 2, 0))
    imag_part = jnp.transpose(imag_part.reshape(each, device_count, rows_here), (1, 2, 0))
    real_part, imag_part = (
        lax.all_to_all(real_part, ("rows", "cols"), split_axis=0, concat_axis=2, tiled=True),
        lax.all_to_all(imag_part, ("rows", "cols"), split_axis=0, concat_axis=2, tiled=True),
    )
    return (real_part.reshape(rows_here, length), imag_part.reshape(rows_here, length))


def chirp_line(index, length):
    square = index * index % (2 * length)
    angle = -(math.pi / length) * square.astype(jnp.float32)
    return (jnp.cos(angle), jnp.sin(angle))


def multiply(real_part, imag_part, other_real, other_imag):
    return (
        real_part * other_real - imag_part * other_imag,
        real_part * other_imag + imag_part * other_real,
    )


def spectral_pair(real_part, imag_part, table_real, table_imag, backward, precision):
    rows_here, length = real_part.shape
    blocks = length // RADIX
    outer = jnp.arange(blocks, dtype=jnp.int32)
    inner = jnp.arange(RADIX, dtype=jnp.int32)
    real_part = real_part.reshape(rows_here, blocks, RADIX)
    imag_part = imag_part.reshape(rows_here, blocks, RADIX)
    cos_outer, sin_outer = phase_pair(outer, outer, blocks)
    cos_mid, sin_mid = phase_pair(outer, inner, length)
    cos_inner, sin_inner = phase_pair(inner, inner, RADIX)
    real_part, imag_part = complex_apply(
        "mab,ak->mkb", real_part, imag_part, cos_outer, sin_outer, False, precision
    )
    real_part, imag_part = twiddle(real_part, imag_part, cos_mid, sin_mid, False)
    real_part, imag_part = complex_apply(
        "mkb,bj->mkj", real_part, imag_part, cos_inner, sin_inner, False, precision
    )
    real_part, imag_part = multiply(real_part, imag_part, table_real, table_imag)
    real_part, imag_part = complex_apply(
        "mkj,jb->mkb", real_part, imag_part, cos_inner, sin_inner, backward, precision
    )
    real_part, imag_part = twiddle(real_part, imag_part, cos_mid, sin_mid, backward)
    real_part, imag_part = complex_apply(
        "mkb,ka->mab", real_part, imag_part, cos_outer, sin_outer, backward, precision
    )
    return (real_part.reshape(rows_here, length), imag_part.reshape(rows_here, length))


def tile_to_columns(part):
    wide = lax.all_to_all(part, "rows", split_axis=1, concat_axis=0, tiled=True)
    return jnp.transpose(wide)


def columns_to_rows(real_part, imag_part):
    each, length = real_part.shape
    row_count, col_count = lax.axis_size("rows"), lax.axis_size("cols")
    device_count = row_count * col_count
    rows_here = length // device_count

    def send(part):
        part = part.reshape(each, row_count, col_count, rows_here)
        part = jnp.transpose(part, (2, 1, 3, 0)).reshape(device_count, rows_here, each)
        part = lax.all_to_all(part, ("cols", "rows"), split_axis=0, concat_axis=2, tiled=True)
        return part.reshape(rows_here, length)

    return (send(real_part), send(imag_part))


def per_device(field_real, field_imag, kerr_map, pinhole):
    real_part, imag_part, phase_one = kerr_phase(field_real, field_imag, kerr_map)
    real_part, imag_part = tile_to_columns(real_part), tile_to_columns(imag_part)
    kerr_wide = lax.all_to_all(kerr_map, "cols", split_axis=0, concat_axis=1, tiled=True)
    length, each = pinhole.shape
    blocks = length // RADIX
    scale = 1.0 / length
    split_index = (
        jnp.arange(blocks, dtype=jnp.int32)[:, None]
        + blocks * jnp.arange(RADIX, dtype=jnp.int32)[None, :]
    )
    line_cos, line_sin = chirp_line(split_index, length)
    line_cos, line_sin = line_cos * scale, line_sin * scale
    own = lax.axis_index(("rows", "cols")) * each + jnp.arange(each, dtype=jnp.int32)
    own_cos, own_sin = chirp_line(own, length)
    own_cos, own_sin = own_cos[:, None, None], own_sin[:, None, None]
    aperture = jnp.transpose(pinhole.reshape(RADIX, blocks, each), (2, 1, 0)).astype(jnp.float32)
    table_real, table_imag = multiply(line_cos[None], line_sin[None], own_cos, own_sin)
    table_real, table_imag = table_real * aperture, table_imag * aperture
    real_part, imag_part = spectral_pair(real_part, imag_part, line_cos, line_sin, True, lax.Precision.HIGHEST)
    real_part, imag_part = columns_to_rows(real_part, imag_part)
    real_part, imag_part = spectral_pair(real_part, imag_part, line_cos, line_sin, True, lax.Precision.HIGHEST)
    real_part, imag_part, phase_two = kerr_phase(real_part, imag_part, kerr_wide)
    phase_back = lax.all_to_all(phase_two, "cols", split_axis=1, concat_axis=0, tiled=True)
    real_part, imag_part = transform_last(real_part, imag_part, False)
    real_part, imag_part = to_tall(real_part, imag_part)
    real_part, imag_part = spectral_pair(real_part, imag_part, table_real, table_imag, False, lax.Precision.HIGH)
    real_part, imag_part = from_tall(real_part, imag_part)
    real_part, imag_part = transform_last(real_part, imag_part, False)
    out_real, out_imag = (
        lax.all_to_all(real_part, "cols", split_axis=1, concat_axis=0, tiled=True),
        lax.all_to_all(imag_part, "cols", split_axis=1, concat_axis=0, tiled=True),
    )
    return (out_real, out_imag, phase_one + phase_back)


LANES = 128


def as_pair(values):
    high = values.astype(np.float32).astype(jnp.bfloat16)
    low = (values - high.astype(np.float64)).astype(np.float32).astype(jnp.bfloat16)
    return np.stack([high, low])


def phase_of(product, period):
    return 2.0 * np.pi * (product % period) / period


def rows_matrix(angle, scale):
    return as_pair(np.concatenate([np.cos(angle), np.sin(angle)], axis=0) * scale)


def packed(values, tail_width=64):
    half = values.shape[-1] - LANES
    pad = [(0, 0)] * (values.ndim - 1) + [(0, tail_width - half)]
    return values[..., :LANES], np.pad(values[..., LANES:], pad)


def packed_columns(real_rows, imag_rows):
    real_main, real_tail = packed(real_rows)
    imag_main, imag_tail = packed(imag_rows)
    return np.concatenate([real_main, imag_main, real_tail, imag_tail], axis=-1)


def transposed_matrix(angle, scale):
    cosine, sine = np.cos(angle) * scale, np.sin(angle) * scale
    upper = packed_columns(cosine, sine)
    lower = packed_columns(-sine, cosine)
    return as_pair(np.concatenate([upper, lower], axis=0))


def lane_square(angle_in_out, scale):
    cosine, sine = np.cos(angle_in_out) * scale, np.sin(angle_in_out) * scale
    from_real = packed_columns(cosine, -sine)
    from_imag = packed_columns(sine, cosine)
    rows = from_real.shape[0]
    pad = np.zeros((64 - (rows - LANES), from_real.shape[1]))
    return as_pair(np.concatenate(
        [from_real[:LANES], from_imag[:LANES], from_real[LANES:], pad, from_imag[LANES:], pad], axis=0
    ))


def lane_table(angle):
    cosine, sine = np.cos(angle), -np.sin(angle)
    cos_main, cos_tail = packed(cosine)
    sin_main, sin_tail = packed(sine)
    return np.stack([
        cos_main, sin_main,
        np.concatenate([cos_tail, cos_tail], axis=-1),
        np.concatenate([-sin_tail, sin_tail], axis=-1),
    ], axis=1).astype(np.float32)


def column_table(angle):
    return np.concatenate([np.cos(angle), -np.sin(angle)], axis=1).astype(np.float32)


def sign_row():
    lane = lax.broadcasted_iota(jnp.int32, (8, LANES), 1)
    return jnp.where(lane < LANES // 2, -1.0, 1.0).astype(jnp.float32)


def swap(value):
    return pltpu.roll(value, LANES // 2, 1)


class Split:
    def __init__(self, real, imag):
        self.real, self.imag = real, imag

    def __add__(self, other):
        return Split(self.real + other.real, self.imag + other.imag)

    def __sub__(self, other):
        return Split(self.real - other.real, self.imag - other.imag)

    def turn(self, cosine, sine):
        return Split(self.real * cosine - self.imag * sine, self.real * sine + self.imag * cosine)

    def quarter(self):
        return Split(self.imag, -self.real)

    def eighth(self, half):
        return Split((self.real + self.imag) * half, (self.imag - self.real) * half)


class Joint:
    def __init__(self, both, sign):
        self.both, self.sign = both, sign

    def __add__(self, other):
        return Joint(self.both + other.both, self.sign)

    def __sub__(self, other):
        return Joint(self.both - other.both, self.sign)

    def turn(self, cosine, sine):
        return Joint(self.both * cosine + swap(self.both) * (self.sign * sine), self.sign)

    def quarter(self):
        return Joint(swap(self.both) * -self.sign, self.sign)

    def eighth(self, half):
        return self.turn(half, -half)


def short_transform(items):
    count = len(items)
    if count == 1:
        return items
    if count % 4:
        return [items[0] + items[1], items[0] - items[1]]
    quarter = count // 4
    parts = [short_transform(items[index::4]) for index in range(4)]
    out = [None] * count
    for index in range(quarter):
        turned = [parts[0][index]]
        for step in range(1, 4):
            place = step * index
            item = parts[step][index]
            if place == 0:
                turned.append(item)
            elif place * 8 == count:
                turned.append(item.eighth(math.sqrt(0.5)))
            elif place * 4 == count:
                turned.append(item.quarter())
            else:
                angle = -2.0 * math.pi * place / count
                turned.append(item.turn(math.cos(angle), math.sin(angle)))
        first, second, third, fourth = turned
        even, odd = first + third, first - third
        even_two, odd_two = second + fourth, (second - fourth).quarter()
        out[index] = even + even_two
        out[index + quarter] = odd + odd_two
        out[index + 2 * quarter] = even - even_two
        out[index + 3 * quarter] = odd - odd_two
    return out


def halves(value):
    high = value.astype(jnp.bfloat16)
    return high, (value - high.astype(jnp.float32)).astype(jnp.bfloat16)


def product(left_high, left_low, right_high, right_low, dims):
    def one(left, right):
        return lax.dot_general(left, right, (dims, ((), ())), preferred_element_type=jnp.float32)

    return one(left_high, right_high) + one(left_low, right_high) + one(left_high, right_low)


NORMAL = ((1,), (0,))
FLIPPED = ((1,), (1,))


def sine_cosine(angle):
    turns = jnp.floor(angle * (2.0 / math.pi) + 0.5)
    rest = angle - turns * 1.5703125
    rest = rest - turns * 4.837512969970703125e-4
    rest = rest - turns * 7.54978995489188216e-8
    quadrant = turns.astype(jnp.int32)
    square = rest * rest
    sine = rest + rest * square * (-1.6666654611e-1 + square * (8.3321608736e-3 + square * -1.9515295891e-4))
    cosine = 1.0 + square * (-0.5 + square * (4.166664568298827e-2 + square * (-1.388731625493765e-3 + square * 2.443315711809948e-5)))
    odd = (quadrant & 1) == 1
    flip_sine = (quadrant & 2) == 2
    flip_cosine = ((quadrant + 1) & 2) == 2
    first = jnp.where(odd, cosine, sine)
    second = jnp.where(odd, sine, cosine)
    return jnp.where(flip_sine, -first, first), jnp.where(flip_cosine, -second, second)


def across(count, steps, load, store, table=None, parts=(True, True)):
    def step(at, carry):
        row = pl.multiple_of(at * 8, 8)
        sign = sign_row()
        if parts[0]:
            main = short_transform([Split(load(s, 0, row), load(s, 1, row)) for s in range(count)])
            for k in range(count):
                item = main[k]
                if table is not None:
                    item = item.turn(*table(k, row, False))
                store(k, 0, row, item.real)
                store(k, 1, row, item.imag)
        if parts[1]:
            tail = short_transform([Joint(load(s, 2, row), sign) for s in range(count)])
            for k in range(count):
                item = tail[k]
                value = item.both
                if table is not None:
                    cosine, signed = table(k, row, True)
                    value = value * cosine + swap(value) * signed
                store(k, 2, row, value)
        return carry

    lax.fori_loop(0, steps, step, 0)


def lane_lookup(table_ref):
    def look(k, row, tail):
        at = 2 if tail else 0
        return table_ref[k, at:at + 1, :], table_ref[k, at + 1:at + 2, :]

    return look


def column_lookup(table_ref, count):
    def look(k, row, tail):
        cosine = jnp.broadcast_to(table_ref[pl.ds(row, 8), k:k + 1], (8, LANES))
        sine = jnp.broadcast_to(table_ref[pl.ds(row, 8), count + k:count + k + 1], (8, LANES))
        return cosine, (sine * sign_row() if tail else sine)

    return look


def column_product(matrix_ref, value):
    high, low = halves(value)
    both = product(matrix_ref[0], matrix_ref[1], high, low, NORMAL)
    outs = both.shape[0] // 2
    first, second = both[:outs], both[outs:]
    sign = sign_row()[:1]
    if value.shape[1] == LANES:
        return (first - swap(second) * sign,)
    if value.shape[1] == 2 * LANES:
        return first[:, :LANES] + second[:, LANES:], first[:, LANES:] - second[:, :LANES]
    real = first[:, :LANES] + second[:, LANES:2 * LANES]
    imag = first[:, LANES:2 * LANES] - second[:, :LANES]
    tail = first[:, 2 * LANES:] - swap(second[:, 2 * LANES:]) * sign
    return real, imag, tail


def flipped_product(matrix_ref, value):
    high, low = halves(value)
    both = product(matrix_ref[0], matrix_ref[1], high, low, FLIPPED)
    outs = both.shape[0] // 2
    width = both.shape[1] - LANES
    real, imag = both[:outs], both[outs:]
    pieces = [real[:, LANES:], imag[:, LANES:]]
    if width < LANES // 2:
        gap = jnp.zeros((outs, LANES // 2 - width), jnp.float32)
        pieces = [pieces[0], gap, pieces[1], gap]
    return real[:, :LANES], imag[:, :LANES], jnp.concatenate(pieces, axis=1)


def joined(ref, *lead):
    return jnp.concatenate([ref[lead + (plane,)] for plane in range(ref.shape[len(lead)])], axis=-1)


def column_turn(parts, cosine, sine):
    if len(parts) == 1:
        return (parts[0] * cosine + swap(parts[0]) * (sine * sign_row()[:1]),)
    real, imag = parts
    return real * cosine - imag * sine, real * sine + imag * cosine


def pick_column(table_ref, at, rows, count):
    lane = lax.broadcasted_iota(jnp.int32, (rows, 2 * count), 1)
    table = table_ref[...]
    cosine = jnp.sum(jnp.where(lane == at, table, 0.0), axis=1, keepdims=True)
    sine = jnp.sum(jnp.where(lane == at + count, table, 0.0), axis=1, keepdims=True)
    return jnp.broadcast_to(cosine, (rows, LANES)), jnp.broadcast_to(sine, (rows, LANES))


def whole(count):
    return [pl.BlockSpec(memory_space=pltpu.VMEM)] * count


def kernel_call(body, outs, inputs, scratch, kilo=0):
    return pl.pallas_call(
        body,
        out_shape=outs,
        in_specs=whole(len(inputs)),
        out_specs=jax.tree.map(lambda _: pl.BlockSpec(memory_space=pltpu.VMEM), outs),
        scratch_shapes=scratch,
        cost_estimate=pl.CostEstimate(flops=kilo * 10**6, bytes_accessed=10**7, transcendentals=0) if kilo else None,
        compiler_params=pltpu.CompilerParams(vmem_limit_bytes=62 * 1024 * 1024),
    )(*inputs)


class Plan:
    def __init__(self, length, row_count, col_count):
        self.length, self.row_count, self.col_count = length, row_count, col_count
        self.count = row_count * col_count
        self.each = length // self.count
        reach = length // 3 + 8
        near = -(-reach // self.count)
        near = (near + 3) // 4 * 4
        steps = np.arange(self.each)
        self.kept = np.concatenate([steps[:near], steps[self.each - near:]])
        self.keep = len(self.kept)
        self.near = near
        scale = 1.0 / math.sqrt(length)
        index = np.arange(self.each)
        self.full = phase_of(np.outer(index, index), self.each)
        self.cut = phase_of(np.outer(self.kept, index), self.each)
        self.scale = scale
        twist = 2.0 * np.pi * np.outer(np.arange(self.count), index) / length
        self.lane_twist = lane_table(twist)
        self.column_twist = column_table(twist.T)
        self.tall = rows_matrix(self.full, scale)
        self.tall_cut = rows_matrix(self.cut, scale)
        self.tall_back = rows_matrix(self.cut.T, scale)
        self.flip = transposed_matrix(self.full, scale)
        self.flip_cut = transposed_matrix(self.cut, scale)
        self.square = lane_square(self.cut, scale)
        far = np.arange(self.count)[:, None] + self.count * self.kept[None, :]
        self.far_chirp = lane_table(np.pi * (far * far % (2 * length)) / length)

    def slot(self, block):
        return block % self.row_count * self.col_count + block // self.row_count


def first_kernel(plan, x_ref, matrix_ref, twist_ref, out_ref, work_ref):
    count, each = plan.count, plan.each
    part = each // plan.row_count
    planes_here = x_ref.shape[1]

    def step(s, carry):
        planes = [
            jnp.concatenate([x_ref[p, plane, pl.ds(s, part, stride=count), :] for p in range(plan.row_count)], axis=0)
            for plane in range(planes_here)
        ]
        parts = column_product(matrix_ref, jnp.concatenate(planes, axis=-1))
        cosine, sine = pick_column(twist_ref, s, each, count)
        for plane, value in enumerate(column_turn(parts, cosine, sine)):
            work_ref[s, plane] = value
        return carry

    lax.fori_loop(0, count, step, 0)

    def load(s, plane, row):
        return work_ref[s, plane, pl.ds(row, 8), :]

    def store(k, plane, row, value):
        out_ref[k, plane, pl.ds(row, 8), :] = value

    across_planes(count, each // 8, load, store, planes_here)


def across_planes(count, steps, load, store, planes_here):
    if planes_here == 2:
        across(count, steps, load, store, None, (True, False))
    else:
        across(
            count, steps, lambda s, plane, row: load(s, plane - 2, row),
            lambda k, plane, row, value: store(k, plane - 2, row, value), None, (False, True),
        )


def second_kernel(plan, x_ref, tail_ref, kerr_ref, theta_ref, own_ref, flip_ref, cut_ref, lane_ref, column_ref,
                  out_ref, phase_ref, work_ref, field_ref):
    count, each = plan.count, plan.each

    def load(s, plane, row):
        if plane == 2:
            return tail_ref[plan.slot(s), 0, pl.ds(row, 8), :]
        return x_ref[plan.slot(s), plane, pl.ds(row, 8), :]

    def store(k, plane, row, value):
        work_ref[k, plane, pl.ds(row, 8), :] = value

    across(count, each // 8, load, store, lane_lookup(lane_ref))

    def turn(k, carry):
        for plane, value in enumerate(flipped_product(flip_ref, joined(work_ref, k))):
            field_ref[plane, pl.ds(k, each, stride=count), :] = value
        return carry

    lax.fori_loop(0, count, turn, 0)
    size = 32

    def kerr(at, carry):
        rows = pl.ds(pl.multiple_of(at * size, size), size)
        sign = sign_row()[:1]
        theta = theta_ref[rows, :]
        real, imag, tail = field_ref[0, rows, :], field_ref[1, rows, :], field_ref[2, rows, :]
        phase = kerr_ref[0, rows, :] * (real * real + imag * imag)
        phase_ref[0, rows, :] = phase
        sine, cosine = sine_cosine(phase + (theta + own_ref[0:1, :]))
        field_ref[0, rows, :] = real * cosine - imag * sine
        field_ref[1, rows, :] = real * sine + imag * cosine
        square = tail * tail
        phase = kerr_ref[1, rows, :] * (square + swap(square))
        phase_ref[1, rows, :] = phase
        sine, cosine = sine_cosine(phase + (theta + own_ref[1:2, :]))
        field_ref[2, rows, :] = tail * cosine + swap(tail) * (sine * sign)
        return carry

    lax.fori_loop(0, plan.length // size, kerr, 0)

    def again(s, plane, row):
        return field_ref[plane, pl.ds(s * each + row, 8), :]

    across(count, each // 8, again, store, column_lookup(column_ref, count))

    def send(k, carry):
        for plane, value in enumerate(column_product(cut_ref, joined(work_ref, k))):
            out_ref[k, plane] = value
        return carry

    lax.fori_loop(0, count, send, 0)


def third_kernel(plan, x_ref, matrix_ref, lane_ref, out_ref, work_ref):
    def load(s, plane, row):
        return x_ref[s, plane, pl.ds(row, 8), :]

    def store(k, plane, row, value):
        work_ref[k, plane, pl.ds(row, 8), :] = value

    across(plan.count, plan.keep // 8, load, store, lane_lookup(lane_ref))

    keep, extra = plan.keep, plan.keep - LANES

    def send(k, carry):
        value = joined(work_ref, k)
        high, low = halves(value[:LANES])
        both = product(matrix_ref[0], matrix_ref[1], high, low, FLIPPED)
        out_ref[k, 0:2 * keep, :] = both
        rest = jnp.concatenate([value[LANES:], jnp.zeros((16 - extra, value.shape[1]), jnp.float32)], axis=0)
        high, low = halves(rest)
        gap = jnp.zeros((extra, LANES - extra), jnp.float32)
        for part in range(2):
            rows = slice(part * keep, (part + 1) * keep)
            tail = product(high, low, matrix_ref[0, rows, :], matrix_ref[1, rows, :], FLIPPED)[:extra]
            at = 2 * keep + 2 * part * extra
            out_ref[k, at:at + extra, :] = tail[:, :LANES]
            out_ref[k, at + extra:at + 2 * extra, :] = jnp.concatenate([tail[:, LANES:], gap], axis=1)
        return carry

    lax.fori_loop(0, plan.count, send, 0)


def fourth_kernel(plan, x_ref, mask_ref, own_ref, chirp_ref, matrix_ref, lane_ref, out_ref, tail_ref, work_ref):
    def step(d, carry):
        sign = sign_row()[:1]
        own_cos, own_sin = own_ref[0], own_ref[1]
        main, tail_mask = mask_ref[d, 0], mask_ref[d, 1]
        far = chirp_ref[d]
        cosine = (own_cos * far[0:1] - own_sin * far[1:2]) * main
        sine = (own_cos * far[1:2] + own_sin * far[0:1]) * main
        keep, extra = plan.keep, plan.keep - LANES
        real, imag = x_ref[d, 0:keep, :], x_ref[d, keep:2 * keep, :]
        gap = jnp.zeros((LANES // 2 - extra, 2 * LANES), jnp.float32)
        pieces = []
        for part in range(2):
            at = 2 * keep + 2 * part * extra
            pieces.append(jnp.concatenate([x_ref[d, at:at + extra, :], x_ref[d, at + extra:at + 2 * extra, :]], axis=1))
            pieces.append(gap)
        tail = jnp.transpose(jnp.concatenate(pieces, axis=0))[:keep]
        own_tail = own_sin * sign
        tail = tail * (own_cos * tail_mask) + swap(tail) * (own_tail * tail_mask)
        tail = tail * far[2:3] + swap(tail) * far[3:4]
        value = jnp.concatenate([real * cosine - imag * sine, real * sine + imag * cosine, tail], axis=-1)
        high, low = halves(value)
        both = product(high, low, matrix_ref[0], matrix_ref[1], NORMAL)
        real, imag, tail = both[:, :LANES], both[:, LANES:2 * LANES], both[:, 2 * LANES:]
        twist = lane_ref[d]
        work_ref[d, 0] = real * twist[0:1] - imag * twist[1:2]
        work_ref[d, 1] = real * twist[1:2] + imag * twist[0:1]
        work_ref[d, 2] = tail * twist[2:3] + swap(tail) * twist[3:4]
        return carry

    lax.fori_loop(0, plan.count, step, 0)

    def load(s, plane, row):
        return work_ref[s, plane, pl.ds(row, 8), :]

    def store(k, plane, row, value):
        if plane == 2:
            tail_ref[plan.slot(k), 0, pl.ds(row, 8), :] = value
        else:
            out_ref[plan.slot(k), plane, pl.ds(row, 8), :] = value

    across(plan.count, plan.keep // 8, load, store)


def fifth_kernel(plan, x_ref, matrix_ref, column_ref, out_ref, work_ref):
    def step(e, carry):
        parts = column_product(matrix_ref, joined(x_ref, e))
        cosine, sine = pick_column(column_ref, e, plan.each, plan.count)
        for plane, value in enumerate(column_turn(parts, cosine, sine)):
            work_ref[e, plane] = value
        return carry

    lax.fori_loop(0, plan.count, step, 0)

    def load(s, plane, row):
        return work_ref[s, plane, pl.ds(row, 8), :]

    def store(k, plane, row, value):
        out_ref[k, plane, pl.ds(row, 8), :] = value

    across_planes(plan.count, plan.each // 8, load, store, x_ref.shape[1])


def f32(*shape):
    return jax.ShapeDtypeStruct(shape, jnp.float32)


def scratch(*shape):
    return pltpu.VMEM(shape, jnp.float32)


def square_angle(index, length):
    return (math.pi / length) * (index * index % (2 * length)).astype(jnp.float32)


def pack_kernel(plan, real_ref, imag_ref, kerr_ref, down_ref, along_ref, out_ref, tail_ref):
    size = 16
    pairs = plan.row_count // 2

    def step(at, carry):
        rows = pl.ds(pl.multiple_of(at * size, size), size)
        low = lax.broadcasted_iota(jnp.int32, (size, LANES), 1) < LANES // 2
        down = down_ref[rows, :]
        for pair in range(pairs):
            tiles = []
            for tile in range(3):
                lanes = slice((3 * pair + tile) * LANES, (3 * pair + tile + 1) * LANES)
                real, imag = real_ref[rows, lanes], imag_ref[rows, lanes]
                phase = kerr_ref[rows, lanes] * (real * real + imag * imag)
                sine, cosine = sine_cosine(phase + (down + along_ref[0:1, lanes]))
                tiles.append((real * cosine - imag * sine, real * sine + imag * cosine))
            (real_a, imag_a), (real_b, imag_b), (real_c, imag_c) = tiles
            even, odd = 2 * pair, 2 * pair + 1
            out_ref[even, 0, rows, :] = real_a
            out_ref[even, 1, rows, :] = imag_a
            tail_ref[even, 0, rows, :] = jnp.where(low, real_b, swap(imag_b))
            turned = swap(real_c)
            out_ref[odd, 0, rows, :] = jnp.where(low, swap(real_b), turned)
            out_ref[odd, 1, rows, :] = jnp.where(low, swap(imag_b), swap(imag_c))
            tail_ref[odd, 0, rows, :] = jnp.where(low, turned, imag_c)
        return carry

    lax.fori_loop(0, real_ref.shape[0] // size, step, 0)


def pack_field(plan, field_real, field_imag, kerr_map, down, along):
    rows_here, cols_here = field_real.shape
    rows = rows_here // plan.col_count
    tile = pl.BlockSpec((rows, cols_here), lambda i: (i, 0))
    return pl.pallas_call(
        functools.partial(pack_kernel, plan),
        out_shape=(f32(plan.row_count, 2, rows_here, LANES), f32(plan.row_count, 1, rows_here, LANES)),
        grid=(plan.col_count,),
        in_specs=[tile, tile, tile, pl.BlockSpec((rows, LANES), lambda i: (i, 0)), pl.BlockSpec((1, cols_here), lambda i: (0, 0))],
        out_specs=tuple(pl.BlockSpec((plan.row_count, planes, rows, LANES), lambda i: (0, 0, i, 0)) for planes in (2, 1)),
        compiler_params=pltpu.CompilerParams(vmem_limit_bytes=40 * 1024 * 1024),
    )(field_real, field_imag, kerr_map, jnp.broadcast_to(down[:, None], (rows_here, LANES)), along[None, :])


def unpack_kernel(plan, field_ref, tail_ref, real_ref, imag_ref):
    size = 16

    def step(at, carry):
        rows = pl.ds(pl.multiple_of(at * size, size), size)
        low = lax.broadcasted_iota(jnp.int32, (size, LANES), 1) < LANES // 2
        for pair in range(plan.row_count // 2):
            even, odd = 2 * pair, 2 * pair + 1
            tails = tail_ref[even, 0, 0, rows, :], tail_ref[odd, 0, 0, rows, :]
            for plane, out_ref in enumerate((real_ref, imag_ref)):
                own = tails[0] if plane == 0 else swap(tails[0])
                last = swap(tails[1]) if plane == 0 else tails[1]
                turned = swap(field_ref[odd, 0, plane, rows, :])
                at_lane = 3 * pair * LANES
                out_ref[rows, at_lane:at_lane + LANES] = field_ref[even, 0, plane, rows, :]
                out_ref[rows, at_lane + LANES:at_lane + 2 * LANES] = jnp.where(low, own, turned)
                out_ref[rows, at_lane + 2 * LANES:at_lane + 3 * LANES] = jnp.where(low, turned, last)
        return carry

    lax.fori_loop(0, real_ref.shape[0] // size, step, 0)


def unpack_field(plan, field, tail, rows_here, cols_here):
    tile = pl.BlockSpec((plan.each, cols_here), lambda i: (i, 0))
    return pl.pallas_call(
        functools.partial(unpack_kernel, plan),
        out_shape=(f32(rows_here, cols_here), f32(rows_here, cols_here)),
        grid=(plan.col_count,),
        in_specs=[pl.BlockSpec((plan.row_count, 1, planes, plan.each, LANES), lambda i: (0, i, 0, 0, 0)) for planes in (2, 1)],
        out_specs=(tile, tile),
        compiler_params=pltpu.CompilerParams(vmem_limit_bytes=40 * 1024 * 1024),
    )(field, tail)


def spread(plan, part, col_at):
    count = plan.col_count
    got = []
    for shift in range(count):
        block = lax.dynamic_index_in_dim(part, (col_at + shift) % count, 0, keepdims=True)
        if shift:
            block = lax.ppermute(block, "cols", [(z, (z + shift) % count) for z in range(count)])
        got.append(block)
    ring = got[::-1]
    return lax.dynamic_slice_in_dim(jnp.concatenate(ring + ring, axis=0), count - 1 - col_at, count, axis=0)


def fast_device(plan, field_real, field_imag, kerr_map, pinhole):
    length, count, each, keep = plan.length, plan.count, plan.each, plan.keep
    rows_here, cols_here = field_real.shape
    row_at, col_at = lax.axis_index("rows"), lax.axis_index("cols")
    own = row_at * plan.col_count + col_at
    both_axes = ("rows", "cols")
    index = jnp.arange(length, dtype=jnp.int32)
    theta = square_angle(index, length)

    phase_one = kerr_map * (field_real * field_real + field_imag * field_imag)
    down = lax.dynamic_slice(theta, (row_at * rows_here,), (rows_here,))
    along = lax.dynamic_slice(theta, (col_at * cols_here,), (cols_here,))
    main, tail = pack_field(plan, field_real, field_imag, kerr_map, down, along)
    tail = lax.all_to_all(tail, "rows", split_axis=0, concat_axis=0, tiled=True)
    main, tail, kerr_here = lax.optimization_barrier((main, tail, kerr_map))
    main = lax.all_to_all(main, "rows", split_axis=0, concat_axis=0, tiled=True)
    kerr = spread(plan, kerr_here.reshape(plan.col_count, each, cols_here), col_at)
    kerr = jnp.transpose(kerr, (0, 2, 1)).reshape(length, each)
    kerr = jnp.stack([kerr[:, :LANES], jnp.concatenate([kerr[:, LANES:], kerr[:, LANES:]], axis=-1)])

    near = plan.near

    def cut(part, axis):
        size = part.shape[axis]
        return jnp.concatenate([
            lax.slice_in_dim(part, 0, near, axis=axis), lax.slice_in_dim(part, size - near, size, axis=axis)
        ], axis=axis)

    mask = jnp.transpose(cut(pinhole.reshape(each, count, each), 0), (1, 0, 2)).astype(jnp.float32)

    theta_wide = jnp.broadcast_to(theta[:, None] - math.pi / 2, (length, LANES))
    lines = lax.dynamic_slice(theta, (own * each,), (each,))
    own_theta = jnp.stack([lines[:LANES], jnp.concatenate([lines[LANES:], lines[LANES:]])])
    far = own + count * jnp.asarray(plan.kept, jnp.int32)
    far_angle = square_angle(far, length)
    own_chirp = jnp.broadcast_to(jnp.stack([jnp.cos(far_angle), -jnp.sin(far_angle)])[:, :, None], (2, keep, LANES))

    def exchange(part):
        return lax.all_to_all(part, both_axes, split_axis=0, concat_axis=0, tiled=True)

    def first(part):
        return kernel_call(
            functools.partial(first_kernel, plan), f32(count, part.shape[1], each, LANES),
            (part, plan.tall, plan.column_twist), [scratch(count, part.shape[1], each, LANES)], 40000,
        )

    tail = first(tail)
    main, tail, kerr = lax.optimization_barrier((main, tail, kerr))
    tail = exchange(tail)
    main = first(main)
    main, tail, mask = lax.optimization_barrier((main, tail, mask))
    main = exchange(main)
    main, mask = lax.optimization_barrier((main, mask))
    mask = lax.all_to_all(mask, both_axes, split_axis=0, concat_axis=0, tiled=True)
    field, phase_two = kernel_call(
        functools.partial(second_kernel, plan),
        (f32(count, 3, keep, LANES), f32(2, length, LANES)),
        (main, tail, kerr, theta_wide, own_theta, plan.flip, plan.tall_cut, plan.lane_twist, plan.column_twist),
        [scratch(count, 3, each, LANES), scratch(3, length, LANES)],
    )
    field, mask = lax.optimization_barrier((field, mask))
    field = exchange(field)
    mask = jnp.transpose(mask, (1, 0, 2)).reshape(keep, each, count)
    mask = jnp.transpose(cut(mask, 1), (2, 0, 1))
    tail = jnp.pad(mask[..., LANES:], ((0, 0), (0, 0), (0, LANES // 2 - (keep - LANES))))
    mask = jnp.stack([mask[..., :LANES], jnp.concatenate([tail, tail], axis=-1)], axis=1)
    field = kernel_call(
        functools.partial(third_kernel, plan), f32(count, 2 * keep + 4 * (keep - LANES), LANES),
        (field, plan.flip_cut, plan.lane_twist), [scratch(count, 3, keep, LANES)],
    )
    field = exchange(field)
    field = kernel_call(
        functools.partial(fourth_kernel, plan), (f32(count, 2, keep, LANES), f32(count, 1, keep, LANES)),
        (field, mask, own_chirp, plan.far_chirp, plan.square, plan.lane_twist), [scratch(count, 3, keep, LANES)],
    )
    main, tail = field
    tail = exchange(tail)
    main, tail = lax.optimization_barrier((main, tail))
    field = exchange(main), tail
    phase = jnp.concatenate([phase_two[0], phase_two[1][:, :LANES // 2]], axis=-1)
    phase = jnp.transpose(phase.reshape(plan.col_count, cols_here, each), (0, 2, 1))

    def last(part):
        part = kernel_call(
            functools.partial(fifth_kernel, plan), f32(count, part.shape[1], each, LANES),
            (part, plan.tall_back, plan.column_twist), [scratch(count, part.shape[1], each, LANES)], 40000,
        )
        return part.reshape(plan.row_count, plan.col_count, part.shape[1], each, LANES)

    main, tail = field
    tail = last(tail)
    main, tail, phase = lax.optimization_barrier((main, tail, phase))
    phase = spread(plan, phase, col_at)
    tail = lax.all_to_all(tail, "rows", split_axis=0, concat_axis=0, tiled=True)
    main = last(main)
    main, tail = lax.optimization_barrier((main, tail))
    main = lax.all_to_all(main, "rows", split_axis=0, concat_axis=0, tiled=True)
    out_real, out_imag = unpack_field(plan, main, tail, rows_here, cols_here)
    return (out_real, out_imag, phase_one + phase.reshape(rows_here, cols_here))


def suits(length, count):
    each = length // count
    return count == 32 and each - LANES == LANES // 2


def solution(mesh):
    placed = (P("rows", "cols"), P("rows", "cols"), P("rows", "cols"), P(None, ("rows", "cols")))

    def device(field_real, field_imag, kerr_map, pinhole):
        row_count, col_count = mesh.shape["rows"], mesh.shape["cols"]
        length = pinhole.shape[0]
        if suits(length, row_count * col_count):
            plan = Plan(length, row_count, col_count)
            return fast_device(plan, field_real, field_imag, kerr_map, pinhole)
        return per_device(field_real, field_imag, kerr_map, pinhole)

    return jax.shard_map(
        device,
        mesh=mesh,
        in_specs=placed,
        out_specs=(P("rows", "cols"), P("rows", "cols"), P("rows", "cols")),
        check_vma=False,
    )
```
